256 devices in a mesh: grp: 8 (over x_lo, y), slab: 32 (over x_hi, z, core).
Axes of the slice: x: 4 (x_hi: 2, x_lo: 2; x = x_hi * 2 + x_lo), y: 4, z: 8, core: 2. Of those that a mesh axis runs over, the one named last changes fastest.
Arguments:
- template: float32 [256, 64, 256], P('slab'), may hold values from -6 to 6
- images: bfloat16 [32, 256, 64, 256], P('grp', 'slab'), may hold values from -6 to 6
- velocity: float32 [32, 3, 256, 64, 256], P('grp', None, 'slab'), may hold values from -3 to 3
- labels: int32 [256, 64, 256], P('slab'), may hold values from 0 to 3
- stiffness: float32 [4], replicated, may hold values from 0.5 to 2
- cohort: int32 [32], P('grp'), may hold values from 0 to 7
- site_gain: float32 [8], replicated, may hold values from 0.5 to 2
Outputs:
- new_template: float32 [256, 64, 256], P('slab')
- new_velocity: float32 [32, 3, 256, 64, 256], P('grp', None, 'slab')
The draws below stay inside these ranges and needn't reach their ends.
All inputs are finite; a program needn't handle non-finite values.
Results may differ from the reference program's by a relative error of at most 0.0003.
Values sent between devices are 32-bit elements; how exact they have to be, the bound alone decides.
No kernel may reach another device: no remote copies, remote signals or barrier semaphores. Data moves between devices by JAX's collectives and lax.ppermute only.
A program may use at most 64 MiB of HBM per device.

```python
import math
import jax
import jax.numpy as jnp
from jax import lax

NY = 64
NX = 256
NLAB = 4
NCOH = 8
NZ = 256
SUBJ = 32


def plant(array, own_key, smallest, top_value):
    longest = array.shape.index(max(array.shape))
    spots = []
    for shift in (0, 1):
        where = [jax.random.randint(jax.random.fold_in(own_key, axis), (), 0, length) for axis, length in enumerate(array.shape)]
        where[longest] = (where[longest] + shift) % array.shape[longest]
        spots.append(tuple(where))
    return array.at[spots[0]].set(smallest).at[spots[1]].set(top_value)


def block_scale(rng, shape, split, low, largest):
    level, own = 1.0, jax.random.fold_in(rng, 6)
    for axis_at, parts in split:
        heights = jnp.exp(jax.random.uniform(jax.random.fold_in(own, axis_at), (parts,), jnp.float32, low / len(split), largest / len(split)))
        level = level * jnp.repeat(heights, shape[axis_at] // parts).reshape([-1 if axis == axis_at else 1 for axis in range(len(shape))])
    return level


def scatter_about(stream_key, extent, width, limit, pieces=(), kind=jnp.bfloat16):
    array = width * jax.random.normal(stream_key, extent, jnp.float32)
    if pieces:
        array = array * block_scale(stream_key, extent, pieces, -0.22, 0.18)
    return jnp.clip(array, -limit, limit).astype(kind)


def setup_inputs(seed: int = 0) -> dict:
    arg_keys = jax.random.split(jax.random.key(seed), 8)
    template = scatter_about(arg_keys[0], (NZ, NY, NX), 1.0, 6.0, ((0, 32),), jnp.float32)
    images = scatter_about(arg_keys[1], (SUBJ, NZ, NY, NX), 1.0, 6.0, ((0, 8), (1, 32)))
    velocity = scatter_about(arg_keys[2], (SUBJ, 3, NZ, NY, NX), 0.5, 3.0, ((0, 8), (2, 32)), jnp.float32)
    labels = plant(jax.random.randint(arg_keys[3], (NZ, NY, NX), 0, NLAB), jax.random.fold_in(arg_keys[3], 1), 0, NLAB - 1).astype(jnp.int32)
    stiffness = jnp.clip(jnp.exp(jax.random.uniform(arg_keys[4], (NLAB,), jnp.float32, math.log(0.5), math.log(2.0))), 0.5, 2.0)
    cohort = plant(jax.random.randint(arg_keys[5], (SUBJ,), 0, NCOH), jax.random.fold_in(arg_keys[5], 1), 0, NCOH - 1).astype(jnp.int32)
    site_gain = jnp.clip(jnp.exp(jax.random.uniform(arg_keys[6], (NCOH,), jnp.float32, math.log(0.5), math.log(2.0))), 0.5, 2.0)
    return dict(template=template, images=images, velocity=velocity, labels=labels, stiffness=stiffness, cohort=cohort, site_gain=site_gain)


velocity_step = 0.05
template_step = 0.5


def slopes_of(padded):
    along_z = 0.5 * (padded[..., 2:, 1:-1, 1:-1] - padded[..., :-2, 1:-1, 1:-1])
    along_y = 0.5 * (padded[..., 1:-1, 2:, 1:-1] - padded[..., 1:-1, :-2, 1:-1])
    along_x = 0.5 * (padded[..., 1:-1, 1:-1, 2:] - padded[..., 1:-1, 1:-1, :-2])
    return jnp.stack([along_z, along_y, along_x], axis=-4)


def around_of(padded):
    beside_all = padded[..., 2:, 1:-1, 1:-1] + padded[..., :-2, 1:-1, 1:-1]
    beside_all = beside_all + padded[..., 1:-1, 2:, 1:-1] + padded[..., 1:-1, :-2, 1:-1]
    return beside_all + padded[..., 1:-1, 1:-1, 2:] + padded[..., 1:-1, 1:-1, :-2]


def reference(template, images, velocity, labels, stiffness, cohort, site_gain):
    slopes = slopes_of(jnp.pad(template, 1))
    stiff_map = stiffness[labels]
    subject_gain = site_gain[cohort]

    def per_subject(running, inputs):
        image, field, gain = inputs
        residual = template + jnp.sum(slopes * field, axis=0) - gain * image.astype(jnp.float32)
        padded = jnp.pad(field, ((0, 0), (1, 1), (1, 1), (1, 1)))
        elastic = stiff_map * (6.0 * field - around_of(padded))
        moved = field - velocity_step * (residual[None] * slopes + elastic)
        return running + residual, moved

    summed, new_velocity = lax.scan(per_subject, jnp.zeros(template.shape, jnp.float32), (images, velocity, subject_gain))
    return template - template_step * summed / SUBJ, new_velocity
```

```python
import functools

import jax
import jax.numpy as jnp
from jax import lax
from jax.experimental import pallas as pl
from jax.experimental.pallas import tpu as pltpu
from jax.sharding import PartitionSpec as P

velocity_step = 0.05
template_step = 0.5
ROWS = 16
MIB = 1 << 20


def beside_y(get_row, here, first, last, count, start):
    rows, width = here.shape
    at = lax.broadcasted_iota(jnp.int32, (rows, width), 0)
    zero = jnp.zeros((rows, width), jnp.float32)
    before = zero if first else jnp.broadcast_to(get_row(start - 1), (rows, width))
    after = zero if last else jnp.broadcast_to(get_row(start + rows), (rows, width))
    lower = jnp.where(at == 0, before, pltpu.roll(here, 1, 0))
    upper = jnp.where(at == rows - 1, after, pltpu.roll(here, rows - 1, 0))
    return lower, upper


def beside_x(here):
    rows, width = here.shape
    at = lax.broadcasted_iota(jnp.int32, (rows, width), 1)
    zero = jnp.zeros((rows, width), jnp.float32)
    lower = jnp.where(at == 0, zero, pltpu.roll(here, 1, 1))
    upper = jnp.where(at == width - 1, zero, pltpu.roll(here, width - 1, 1))
    return lower, upper


def plane_slopes(t_ref, z, j, below, above):
    count = t_ref.shape[1]
    start = j * ROWS
    rows = pl.ds(start, ROWS)
    here = t_ref[z, rows, :]
    y_low, y_high = beside_y(
        lambda at: t_ref[z, pl.ds(at, 1), :], here, j == 0, start + ROWS == count, count, start
    )
    x_low, x_high = beside_x(here)
    return 0.5 * (above - below), 0.5 * (y_high - y_low), 0.5 * (x_high - x_low)


def partial_kernel(cohort, gain, t_ref, im_ref, v_ref, sum_ref, edge_ref, first_ref, last_ref, s_ref):
    subject = pl.program_id(0)
    depth, count, width = t_ref.shape
    chunks = count // ROWS
    level = gain[cohort[subject]]

    @pl.when(subject == 0)
    def _():
        for j in range(chunks):
            rows = pl.ds(j * ROWS, ROWS)
            zero = jnp.zeros((ROWS, width), jnp.float32)

            def slope(z, below, above):
                for c, value in enumerate(plane_slopes(t_ref, z, j, below, above)):
                    s_ref[c, z, rows, :] = value

            slope(0, zero, t_ref[1, rows, :])
            slope(depth - 1, t_ref[depth - 2, rows, :], zero)

            @pl.loop(1, depth - 1)
            def _(z):
                slope(z, t_ref[z - 1, rows, :], t_ref[z + 1, rows, :])

    def accumulate(fresh):
        @pl.loop(0, depth)
        def _(z):
            for j in range(chunks):
                rows = pl.ds(j * ROWS, ROWS)
                value = t_ref[z, rows, :] - level * im_ref[0, z, rows, :].astype(jnp.float32)
                for c in range(3):
                    value = value + s_ref[c, z, rows, :] * v_ref[0, c, z, rows, :]
                if not fresh:
                    value = value + sum_ref[z, rows, :]
                sum_ref[z, rows, :] = value

        for side, z in enumerate((0, depth - 1)):
            if fresh:
                edge_ref[side] = v_ref[0, 0, z]
            else:
                edge_ref[side] = edge_ref[side] + v_ref[0, 0, z]

    pl.when(subject == 0)(lambda: accumulate(True))
    pl.when(subject > 0)(lambda: accumulate(False))
    for c in range(3):
        first_ref[0, c, 0] = v_ref[0, c, 0]
        last_ref[0, c, 0] = v_ref[0, c, depth - 1]


def move_kernel(
    cohort, gain, stiff, t_ref, tl_ref, th_ref, lab_ref, im_ref, v_ref, vl_ref, vh_ref, out_ref, s_ref, k_ref
):
    subject = pl.program_id(0)
    depth, count, width = t_ref.shape
    chunks = count // ROWS
    level = gain[cohort[subject]]

    @pl.when(subject == 0)
    def _():
        for j in range(chunks):
            rows = pl.ds(j * ROWS, ROWS)

            def slope(z, below, above):
                for c, value in enumerate(plane_slopes(t_ref, z, j, below, above)):
                    s_ref[c, z, rows, :] = value
                label = lab_ref[z, rows, :]
                rate = jnp.full((ROWS, width), stiff[0], jnp.float32)
                for kind in range(1, 4):
                    rate = jnp.where(label == kind, stiff[kind], rate)
                k_ref[z, rows, :] = velocity_step * rate

            slope(0, tl_ref[0, rows, :], t_ref[1, rows, :])
            slope(depth - 1, t_ref[depth - 2, rows, :], th_ref[0, rows, :])

            @pl.loop(1, depth - 1)
            def _(z):
                slope(z, t_ref[z - 1, rows, :], t_ref[z + 1, rows, :])

    def plane(z, below, above):
        for j in range(chunks):
            start = j * ROWS
            rows = pl.ds(start, ROWS)
            field = [v_ref[0, c, z, rows, :] for c in range(3)]
            slopes = [s_ref[c, z, rows, :] for c in range(3)]
            rate = k_ref[z, rows, :]
            value = t_ref[z, rows, :] - level * im_ref[0, z, rows, :].astype(jnp.float32)
            for c in range(3):
                value = value + slopes[c] * field[c]
            value = velocity_step * value
            for c in range(3):
                here = field[c]
                y_low, y_high = beside_y(
                    lambda at: v_ref[0, c, z, pl.ds(at, 1), :], here, j == 0, start + ROWS == count, count, start
                )
                x_low, x_high = beside_x(here)
                around = (below(c, rows) + above(c, rows)) + (y_low + y_high) + (x_low + x_high)
                out_ref[0, c, z, rows, :] = here + rate * (around - 6.0 * here) - value * slopes[c]

    plane(0, lambda c, rows: vl_ref[0, c, 0, rows, :], lambda c, rows: v_ref[0, c, 1, rows, :])
    plane(
        depth - 1,
        lambda c, rows: v_ref[0, c, depth - 2, rows, :],
        lambda c, rows: vh_ref[0, c, 0, rows, :],
    )

    @pl.loop(1, depth - 1)
    def _(z):
        plane(z, lambda c, rows: v_ref[0, c, z - 1, rows, :], lambda c, rows: v_ref[0, c, z + 1, rows, :])


def whole(shape):
    return pl.BlockSpec(shape, lambda *_: (0,) * len(shape))


def per_subject(shape):
    return pl.BlockSpec((1,) + shape[1:], lambda s, *_: (s,) + (0,) * (len(shape) - 1))


def partial_sums(cohort, gain, template, images, velocity):
    subjects = images.shape[0]
    depth, count, width = template.shape
    edge = (subjects, 3, 1, count, width)
    shapes = (template.shape, (2, count, width), edge, edge)
    return pl.pallas_call(
        partial_kernel,
        out_shape=[jax.ShapeDtypeStruct(shape, jnp.float32) for shape in shapes],
        grid_spec=pltpu.PrefetchScalarGridSpec(
            num_scalar_prefetch=2,
            grid=(subjects,),
            in_specs=[whole(template.shape), per_subject(images.shape), per_subject(velocity.shape)],
            out_specs=[whole(shapes[0]), whole(shapes[1]), per_subject(edge), per_subject(edge)],
            scratch_shapes=[pltpu.VMEM((3,) + template.shape, jnp.float32)],
        ),
        compiler_params=pltpu.CompilerParams(vmem_limit_bytes=60 * MIB),
        cost_estimate=pl.CostEstimate(flops=12 * velocity.size, bytes_accessed=10 * MIB, transcendentals=0),
        name="partial_sums",
    )(cohort, gain, template, images, velocity)


def moved(cohort, gain, stiffness, template, t_low, t_high, labels, images, velocity, v_low, v_high):
    subjects = images.shape[0]
    return pl.pallas_call(
        move_kernel,
        out_shape=jax.ShapeDtypeStruct(velocity.shape, jnp.float32),
        grid_spec=pltpu.PrefetchScalarGridSpec(
            num_scalar_prefetch=3,
            grid=(subjects,),
            in_specs=[
                whole(template.shape),
                whole(t_low.shape),
                whole(t_high.shape),
                whole(labels.shape),
                per_subject(images.shape),
                per_subject(velocity.shape),
                per_subject(v_low.shape),
                per_subject(v_high.shape),
            ],
            out_specs=per_subject(velocity.shape),
            scratch_shapes=[
                pltpu.VMEM((3,) + template.shape, jnp.float32),
                pltpu.VMEM(template.shape, jnp.float32),
            ],
        ),
        compiler_params=pltpu.CompilerParams(vmem_limit_bytes=60 * MIB),
        cost_estimate=pl.CostEstimate(flops=25 * velocity.size, bytes_accessed=16 * MIB, transcendentals=0),
        name="moved",
    )(cohort, gain, stiffness, template, t_low, t_high, labels, images, velocity, v_low, v_high)


def local(template, images, velocity, labels, stiffness, cohort, site_gain):
    depth = template.shape[0]
    count = lax.axis_size("slab")
    groups = lax.axis_size("grp")
    forward = [(i, i + 1) for i in range(count - 1)]
    backward = [(i + 1, i) for i in range(count - 1)]
    t_low = lax.ppermute(template[depth - 1 :], "slab", forward)
    t_high = lax.ppermute(template[:1], "slab", backward)
    part, edge, first, last = partial_sums(cohort, site_gain, template, images, velocity)
    v_low = lax.ppermute(last, "slab", forward)
    v_high = lax.ppermute(first, "slab", backward)
    part = jnp.concatenate(
        [
            part[:1] - 0.5 * t_low * edge[:1],
            part[1 : depth - 1],
            part[depth - 1 :] + 0.5 * t_high * edge[1:],
        ],
        axis=0,
    )
    shares = lax.all_to_all(part, "grp", 0, 0, tiled=True)
    own_planes = depth // groups
    summed = jnp.sum(shares.reshape((groups, own_planes) + template.shape[1:]), axis=0)
    own = lax.dynamic_slice_in_dim(template, lax.axis_index("grp") * own_planes, own_planes, 0)
    own = own - template_step * summed / (images.shape[0] * groups)
    new_template = lax.all_to_all(
        jnp.broadcast_to(own[None], (groups,) + own.shape).reshape(template.shape), "grp", 0, 0, tiled=True
    )
    new_velocity = moved(
        cohort, site_gain, stiffness, template, t_low, t_high, labels, images, velocity, v_low, v_high
    )
    return (new_template, new_velocity)


def solution(mesh):
    placed = (
        P("slab", None, None),
        P("grp", "slab", None, None),
        P("grp", None, "slab", None, None),
        P("slab", None, None),
        P(),
        P("grp"),
        P(),
    )
    return jax.shard_map(
        local,
        mesh=mesh,
        in_specs=placed,
        out_specs=(P("slab", None, None), P("grp", None, "slab", None, None)),
        check_vma=False,
    )
```

```python
import jax
import jax.numpy as jnp
from jax import lax
from jax.experimental import pallas as pl
from jax.experimental.pallas import tpu as pltpu
from jax.sharding import PartitionSpec as P

velocity_step = 0.05
template_step = 0.5
ROWS = 16
MIB = 1 << 20


def beside_y(get_row, here, first, last, count, start):
    rows, width = here.shape
    at = lax.broadcasted_iota(jnp.int32, (rows, width), 0)
    zero = jnp.zeros((rows, width), jnp.float32)
    before = zero if first else jnp.broadcast_to(get_row(start - 1), (rows, width))
    after = zero if last else jnp.broadcast_to(get_row(start + rows), (rows, width))
    lower = jnp.where(at == 0, before, pltpu.roll(here, 1, 0))
    upper = jnp.where(at == rows - 1, after, pltpu.roll(here, rows - 1, 0))
    return lower, upper


def beside_x(here):
    rows, width = here.shape
    at = lax.broadcasted_iota(jnp.int32, (rows, width), 1)
    zero = jnp.zeros((rows, width), jnp.float32)
    lower = jnp.where(at == 0, zero, pltpu.roll(here, 1, 1))
    upper = jnp.where(at == width - 1, zero, pltpu.roll(here, width - 1, 1))
    return lower, upper


def fill_slopes(t_ref, s_ref, also=None):
    depth, count, width = s_ref.shape[1:]

    @pl.loop(0, depth)
    def _(z):
        for j in range(count // ROWS):
            start = j * ROWS
            rows = pl.ds(start, ROWS)
            here = t_ref[z + 1, rows, :]
            y_low, y_high = beside_y(
                lambda at: t_ref[z + 1, pl.ds(at, 1), :], here, j == 0, start + ROWS == count, count, start
            )
            x_low, x_high = beside_x(here)
            s_ref[0, z, rows, :] = 0.5 * (t_ref[z + 2, rows, :] - t_ref[z, rows, :])
            s_ref[1, z, rows, :] = 0.5 * (y_high - y_low)
            s_ref[2, z, rows, :] = 0.5 * (x_high - x_low)
            if also is not None:
                also(z, rows)


def template_copies(odd, t_hbm, ti_hbm, to_hbm, t_ref, sem):
    depth = t_hbm.shape[0]
    inner = jnp.where(odd == 1, 0, depth + 1)
    outer = depth + 1 - inner
    return [
        pltpu.make_async_copy(t_hbm, t_ref.at[pl.ds(1, depth)], sem.at[0]),
        pltpu.make_async_copy(ti_hbm, t_ref.at[pl.ds(inner, 1)], sem.at[1]),
        pltpu.make_async_copy(to_hbm, t_ref.at[pl.ds(outer, 1)], sem.at[2]),
    ]


def partial_kernel(
    odd_ref, cohort, gain, t_hbm, ti_hbm, to_hbm, im_hbm, v_hbm, sum_ref, inner_hbm, outer_hbm,
    t_ref, im_ref, v_ref, s_ref, t_sem, im_sem, v_sem, in_sem, out_sem,
):
    subjects, depth, count, width = im_ref.shape
    odd = odd_ref[0]
    template = template_copies(odd, t_hbm, ti_hbm, to_hbm, t_ref, t_sem)
    images = [pltpu.make_async_copy(im_hbm.at[s], im_ref.at[s], im_sem.at[s]) for s in range(subjects)]
    fields = [
        [pltpu.make_async_copy(v_hbm.at[s, c], v_ref.at[s, c], v_sem.at[s, c]) for c in range(3)]
        for s in range(subjects)
    ]
    facing = jnp.where(odd == 1, 0, depth - 1)
    inner = [
        pltpu.make_async_copy(v_ref.at[s, :, pl.ds(facing, 1)], inner_hbm.at[s], in_sem.at[s])
        for s in range(subjects)
    ]
    outer = [
        pltpu.make_async_copy(v_ref.at[s, :, pl.ds(depth - 1 - facing, 1)], outer_hbm.at[s], out_sem.at[s])
        for s in range(subjects)
    ]
    for copy in template:
        copy.start()
    for s in range(subjects):
        images[s].start()
        for copy in fields[s]:
            copy.start()
    for copy in template:
        copy.wait()
    fill_slopes(t_ref, s_ref)
    pair = 2 if subjects % 2 == 0 else 1
    for low in range(0, subjects, pair):
        members = range(low, low + pair)
        for s in members:
            images[s].wait()
            for copy in fields[s]:
                copy.wait()
            inner[s].start()
            outer[s].start()
        levels = [gain[cohort[s]] for s in members]

        @pl.loop(0, depth)
        def _(z):
            for j in range(count // ROWS):
                rows = pl.ds(j * ROWS, ROWS)
                value = float(pair) * t_ref[z + 1, rows, :]
                for s, level in zip(members, levels):
                    value = value - level * im_ref[s, z, rows, :].astype(jnp.float32)
                for c in range(3):
                    field = v_ref[low, c, z, rows, :]
                    for s in members[1:]:
                        field = field + v_ref[s, c, z, rows, :]
                    value = value + s_ref[c, z, rows, :] * field
                if low:
                    value = value + sum_ref[z, rows, :]
                sum_ref[z, rows, :] = value

    for copy in inner + outer:
        copy.wait()


def share_kernel(place, scale, t_hbm, parts_ref, out_ref, own_ref, sem):
    groups, count, width = parts_ref.shape
    copy = pltpu.make_async_copy(t_hbm.at[place[0]], own_ref, sem)
    copy.start()
    copy.wait()
    for j in range(count // ROWS):
        rows = pl.ds(j * ROWS, ROWS)
        total = parts_ref[0, rows, :]
        for g in range(1, groups):
            total = total + parts_ref[g, rows, :]
        value = own_ref[rows, :] - scale * total
        for g in range(groups):
            out_ref[g, rows, :] = value


def move_kernel(
    odd_ref, cohort, gain, stiff, t_hbm, ti_hbm, to_hbm, lab_hbm, im_hbm, v_hbm, vi_hbm, vo_hbm, out_hbm,
    t_ref, lab_ref, im_ref, v_ref, new_ref, s_ref, k_ref,
    t_sem, lab_sem, im_sem, v_sem, vi_sem, vo_sem, out_sem,
):
    subjects, depth, count, width = im_ref.shape
    odd = odd_ref[0]
    template = template_copies(odd, t_hbm, ti_hbm, to_hbm, t_ref, t_sem)
    template.append(pltpu.make_async_copy(lab_hbm, lab_ref, lab_sem))
    inner = jnp.where(odd == 1, 0, depth + 1)
    half = depth // 2

    def arrivals(s):
        copies = [pltpu.make_async_copy(im_hbm.at[s], im_ref.at[s], im_sem.at[s])]
        for c in range(3):
            copies.append(
                pltpu.make_async_copy(v_hbm.at[s, c], v_ref.at[s, c, pl.ds(1, depth)], v_sem.at[s, c])
            )
        copies.append(pltpu.make_async_copy(vi_hbm.at[s], v_ref.at[s, :, pl.ds(inner, 1)], vi_sem.at[s]))
        copies.append(
            pltpu.make_async_copy(vo_hbm.at[s], v_ref.at[s, :, pl.ds(depth + 1 - inner, 1)], vo_sem.at[s])
        )
        return copies

    def departure(s, part):
        planes = pl.ds(part * half, half)
        return pltpu.make_async_copy(new_ref.at[s, :, planes], out_hbm.at[s, :, planes], out_sem.at[s, part])

    for copy in template:
        copy.start()
    for s in range(subjects):
        for copy in arrivals(s):
            copy.start()
    for copy in template:
        copy.wait()

    def rate_of(z, rows):
        label = lab_ref[z, rows, :]
        rate = jnp.full(label.shape, stiff[0], jnp.float32)
        for kind in range(1, stiff.shape[0]):
            rate = jnp.where(label == kind, stiff[kind], rate)
        k_ref[z, rows, :] = velocity_step * rate

    fill_slopes(t_ref, s_ref, rate_of)

    @pl.loop(0, subjects)
    def _(s):
        for copy in arrivals(s):
            copy.wait()
        level = gain[cohort[s]]

        def plane(z):
            for j in range(count // ROWS):
                start = j * ROWS
                rows = pl.ds(start, ROWS)
                field = [v_ref[s, c, z + 1, rows, :] for c in range(3)]
                slopes = [s_ref[c, z, rows, :] for c in range(3)]
                rate = k_ref[z, rows, :]
                value = t_ref[z + 1, rows, :] - level * im_ref[s, z, rows, :].astype(jnp.float32)
                for c in range(3):
                    value = value + slopes[c] * field[c]
                value = velocity_step * value
                for c in range(3):
                    here = field[c]
                    y_low, y_high = beside_y(
                        lambda at: v_ref[s, c, z + 1, pl.ds(at, 1), :], here,
                        j == 0, start + ROWS == count, count, start,
                    )
                    x_low, x_high = beside_x(here)
                    around = (v_ref[s, c, z, rows, :] + v_ref[s, c, z + 2, rows, :]) + (y_low + y_high)
                    around = around + (x_low + x_high)
                    new_ref[s, c, z, rows, :] = here + rate * (around - 6.0 * here) - value * slopes[c]

        for part in range(2):
            pl.loop(part * half, (part + 1) * half)(plane)
            departure(s, part).start()

    @pl.loop(0, subjects)
    def _(s):
        for part in range(2):
            departure(s, part).wait()


SMALL = pl.BlockSpec(memory_space=pltpu.SMEM)
FAR = pl.BlockSpec(memory_space=pltpu.HBM)
FREE = pl.BlockSpec(memory_space=pl.ANY)
NEAR = pl.BlockSpec(memory_space=pltpu.VMEM)
COPY = pltpu.SemaphoreType.DMA


def partial_sums(odd, cohort, gain, template, t_inner, t_outer, images, velocity):
    subjects = images.shape[0]
    depth, count, width = template.shape
    edge = jax.ShapeDtypeStruct((subjects, 3, 1, count, width), jnp.float32)
    return pl.pallas_call(
        partial_kernel,
        out_shape=[jax.ShapeDtypeStruct(template.shape, jnp.float32), edge, edge],
        in_specs=[SMALL] * 3 + [FAR, FREE, FREE, FAR, FAR],
        out_specs=[NEAR, FAR, FAR],
        scratch_shapes=[
            pltpu.VMEM((depth + 2, count, width), jnp.float32),
            pltpu.VMEM(images.shape, images.dtype),
            pltpu.VMEM(velocity.shape, jnp.float32),
            pltpu.VMEM((3,) + template.shape, jnp.float32),
            COPY((3,)), COPY((subjects,)), COPY((subjects, 3)), COPY((subjects,)), COPY((subjects,)),
        ],
        compiler_params=pltpu.CompilerParams(vmem_limit_bytes=60 * MIB),
        cost_estimate=pl.CostEstimate(flops=4 * velocity.size, bytes_accessed=10 * MIB, transcendentals=0),
        name="partial_sums",
    )(odd, cohort, gain, template, t_inner, t_outer, images, velocity)


def share_update(place, scale, template, parts):
    return pl.pallas_call(
        lambda *refs: share_kernel(refs[0], scale, *refs[1:]),
        out_shape=jax.ShapeDtypeStruct(parts.shape, jnp.float32),
        in_specs=[SMALL, FAR, NEAR],
        out_specs=NEAR,
        scratch_shapes=[pltpu.VMEM(template.shape[1:], jnp.float32), COPY(())],
        compiler_params=pltpu.CompilerParams(vmem_limit_bytes=8 * MIB),
        cost_estimate=pl.CostEstimate(flops=parts.size, bytes_accessed=2 * MIB, transcendentals=0),
        name="share_update",
    )(place, template, parts)


def moved(odd, cohort, gain, stiffness, template, t_inner, t_outer, labels, images, velocity, v_inner, v_outer):
    subjects = images.shape[0]
    depth, count, width = template.shape
    return pl.pallas_call(
        move_kernel,
        out_shape=jax.ShapeDtypeStruct(velocity.shape, jnp.float32),
        in_specs=[SMALL] * 4 + [FAR, FREE, FREE, FAR, FAR, FAR, FREE, FREE],
        out_specs=FAR,
        scratch_shapes=[
            pltpu.VMEM((depth + 2, count, width), jnp.float32),
            pltpu.VMEM(labels.shape, labels.dtype),
            pltpu.VMEM(images.shape, images.dtype),
            pltpu.VMEM((subjects, 3, depth + 2, count, width), jnp.float32),
            pltpu.VMEM(velocity.shape, jnp.float32),
            pltpu.VMEM((3,) + template.shape, jnp.float32),
            pltpu.VMEM(template.shape, jnp.float32),
            COPY((3,)), COPY(()), COPY((subjects,)), COPY((subjects, 3)),
            COPY((subjects,)), COPY((subjects,)), COPY((subjects, 2)),
        ],
        compiler_params=pltpu.CompilerParams(vmem_limit_bytes=60 * MIB),
        cost_estimate=pl.CostEstimate(flops=8 * velocity.size, bytes_accessed=16 * MIB, transcendentals=0),
        name="moved",
    )(odd, cohort, gain, stiffness, template, t_inner, t_outer, labels, images, velocity, v_inner, v_outer)


def local(template, images, velocity, labels, stiffness, cohort, site_gain):
    depth = template.shape[0]
    slabs = lax.axis_size("slab")
    groups = lax.axis_size("grp")
    assert depth == groups and slabs % 2 == 0
    odd = lax.axis_index("slab") % 2
    place = lax.axis_index("grp").reshape(1)
    inside = [(i, i ^ 1) for i in range(slabs)]
    across = [(i, i + 1) for i in range(1, slabs - 1, 2)]
    across = across + [(target, source) for source, target in across]
    facing = jnp.where(odd == 1, 0, depth - 1)
    t_inner = lax.ppermute(lax.dynamic_slice_in_dim(template, facing, 1, 0), "slab", inside)
    t_outer = lax.ppermute(lax.dynamic_slice_in_dim(template, depth - 1 - facing, 1, 0), "slab", across)
    odd = odd.reshape(1)
    part, inner, outer = partial_sums(odd, cohort, site_gain, template, t_inner, t_outer, images, velocity)
    v_inner = lax.ppermute(inner, "slab", inside)
    v_outer = lax.ppermute(outer, "slab", across)
    parts = lax.all_to_all(part, "grp", 0, 0, tiled=True)
    shares = share_update(place, template_step / (images.shape[0] * groups), template, parts)
    new_template = lax.all_to_all(shares, "grp", 0, 0, tiled=True)
    new_velocity = moved(
        odd, cohort, site_gain, stiffness, template, t_inner, t_outer, labels, images, velocity, v_inner, v_outer
    )
    return (new_template, new_velocity)


def solution(mesh):
    placed = (
        P("slab", None, None),
        P("grp", "slab", None, None),
        P("grp", None, "slab", None, None),
        P("slab", None, None),
        P(),
        P("grp"),
        P(),
    )
    return jax.shard_map(
        local,
        mesh=mesh,
        in_specs=placed,
        out_specs=(P("slab", None, None), P("grp", None, "slab", None, None)),
        check_vma=False,
    )
```

```python
import jax
import jax.numpy as jnp
from jax import lax
from jax.experimental import pallas as pl
from jax.experimental.pallas import tpu as pltpu
from jax.sharding import PartitionSpec as P

velocity_step = 0.05
template_step = 0.5
ROWS = 16
MIB = 1 << 20


def beside_y(get_row, here, first, last, count, start):
    rows, width = here.shape
    at = lax.broadcasted_iota(jnp.int32, (rows, width), 0)
    zero = jnp.zeros((rows, width), jnp.float32)
    before = zero if first else jnp.broadcast_to(get_row(start - 1), (rows, width))
    after = zero if last else jnp.broadcast_to(get_row(start + rows), (rows, width))
    lower = jnp.where(at == 0, before, pltpu.roll(here, 1, 0))
    upper = jnp.where(at == rows - 1, after, pltpu.roll(here, rows - 1, 0))
    return lower, upper


def beside_x(here):
    rows, width = here.shape
    at = lax.broadcasted_iota(jnp.int32, (rows, width), 1)
    zero = jnp.zeros((rows, width), jnp.float32)
    lower = jnp.where(at == 0, zero, pltpu.roll(here, 1, 1))
    upper = jnp.where(at == width - 1, zero, pltpu.roll(here, width - 1, 1))
    return lower, upper


def fill_slopes(t_ref, s_ref, also=None):
    depth, count, width = s_ref.shape[1:]

    @pl.loop(0, depth)
    def _(z):
        for j in range(count // ROWS):
            start = j * ROWS
            rows = pl.ds(start, ROWS)
            here = t_ref[z + 1, rows, :]
            y_low, y_high = beside_y(
                lambda at: t_ref[z + 1, pl.ds(at, 1), :], here, j == 0, start + ROWS == count, count, start
            )
            x_low, x_high = beside_x(here)
            s_ref[0, z, rows, :] = 0.5 * (t_ref[z + 2, rows, :] - t_ref[z, rows, :])
            s_ref[1, z, rows, :] = 0.5 * (y_high - y_low)
            s_ref[2, z, rows, :] = 0.5 * (x_high - x_low)
            if also is not None:
                also(z, rows)


def template_copies(odd, t_hbm, ti_hbm, to_hbm, t_ref, sem):
    depth = t_hbm.shape[0]
    inner = jnp.where(odd == 1, 0, depth + 1)
    outer = depth + 1 - inner
    return [
        pltpu.make_async_copy(t_hbm, t_ref.at[pl.ds(1, depth)], sem.at[0]),
        pltpu.make_async_copy(ti_hbm, t_ref.at[pl.ds(inner, 1)], sem.at[1]),
        pltpu.make_async_copy(to_hbm, t_ref.at[pl.ds(outer, 1)], sem.at[2]),
    ]


def share_kernel(place, scale, t_hbm, parts_ref, out_ref, own_ref, sem):
    groups, count, width = parts_ref.shape
    copy = pltpu.make_async_copy(t_hbm.at[place[0]], own_ref, sem)
    copy.start()
    copy.wait()
    for j in range(count // ROWS):
        rows = pl.ds(j * ROWS, ROWS)
        total = parts_ref[0, rows, :]
        for g in range(1, groups):
            total = total + parts_ref[g, rows, :]
        value = own_ref[rows, :] - scale * total
        for g in range(groups):
            out_ref[g, rows, :] = value


def move_kernel(
    odd_ref, cohort, gain, stiff, t_hbm, ti_hbm, to_hbm, lab_hbm, im_hbm, v_hbm,
    sum_ref, inner_hbm, outer_hbm, out_hbm,
    t_ref, lab_ref, im_ref, v_ref, new_ref, s_ref, k_ref,
    t_sem, lab_sem, im_sem, v_sem, in_sem, far_sem, out_sem,
):
    subjects, depth, count, width = im_ref.shape
    odd = odd_ref[0]
    template = template_copies(odd, t_hbm, ti_hbm, to_hbm, t_ref, t_sem)
    template.append(pltpu.make_async_copy(lab_hbm, lab_ref, lab_sem))
    facing = jnp.where(odd == 1, 0, depth - 1)
    half = depth // 2

    def arrivals(s):
        copies = [pltpu.make_async_copy(im_hbm.at[s], im_ref.at[s], im_sem.at[s])]
        for c in range(3):
            copies.append(
                pltpu.make_async_copy(v_hbm.at[s, c], v_ref.at[s, c, pl.ds(1, depth)], v_sem.at[s, c])
            )
        return copies

    def edges(s):
        return [
            pltpu.make_async_copy(v_ref.at[s, :, pl.ds(1 + facing, 1)], inner_hbm.at[s], in_sem.at[s]),
            pltpu.make_async_copy(v_ref.at[s, :, pl.ds(depth - facing, 1)], outer_hbm.at[s], far_sem.at[s]),
        ]

    def departure(s, part):
        planes = pl.ds(part * half, half)
        return pltpu.make_async_copy(new_ref.at[s, :, planes], out_hbm.at[s, :, planes], out_sem.at[s, part])

    for copy in template:
        copy.start()
    for s in range(subjects):
        for copy in arrivals(s):
            copy.start()
    sum_ref[...] = jnp.zeros_like(sum_ref)
    outside = jnp.zeros((count, width), jnp.float32)

    @pl.loop(0, subjects)
    def _(s):
        for c in range(3):
            v_ref[s, c, 0] = outside
            v_ref[s, c, depth + 1] = outside

    for copy in template:
        copy.wait()

    def rate_of(z, rows):
        k_ref[z, rows, :] = rate_at(lab_ref[z, rows, :], stiff)

    fill_slopes(t_ref, s_ref, rate_of)

    @pl.loop(0, subjects)
    def _(s):
        for copy in arrivals(s):
            copy.wait()
        for copy in edges(s):
            copy.start()
        level = gain[cohort[s]]

        def plane(z):
            for j in range(count // ROWS):
                start = j * ROWS
                rows = pl.ds(start, ROWS)
                field = [v_ref[s, c, z + 1, rows, :] for c in range(3)]
                slopes = [s_ref[c, z, rows, :] for c in range(3)]
                rate = k_ref[z, rows, :]
                value = t_ref[z + 1, rows, :] - level * im_ref[s, z, rows, :].astype(jnp.float32)
                for c in range(3):
                    value = value + slopes[c] * field[c]
                sum_ref[z, rows, :] = sum_ref[z, rows, :] + value
                value = velocity_step * value
                for c in range(3):
                    here = field[c]
                    y_low, y_high = beside_y(
                        lambda at: v_ref[s, c, z + 1, pl.ds(at, 1), :], here,
                        j == 0, start + ROWS == count, count, start,
                    )
                    x_low, x_high = beside_x(here)
                    around = (v_ref[s, c, z, rows, :] + v_ref[s, c, z + 2, rows, :]) + (y_low + y_high)
                    around = around + (x_low + x_high)
                    new_ref[s, c, z, rows, :] = here + rate * (around - 6.0 * here) - value * slopes[c]

        for part in range(2):
            pl.loop(part * half, (part + 1) * half)(plane)
            departure(s, part).start()

    @pl.loop(0, subjects)
    def _(s):
        for copy in edges(s):
            copy.wait()
        for part in range(2):
            departure(s, part).wait()


def rate_at(label, stiff):
    rate = jnp.full(label.shape, stiff[0], jnp.float32)
    for kind in range(1, stiff.shape[0]):
        rate = jnp.where(label == kind, stiff[kind], rate)
    return velocity_step * rate


def edge_kernel(
    odd_ref, stiff, lab_hbm, vi_ref, vo_ref, old_hbm, out_hbm, lab_ref, near_ref, far_ref,
    lab_sem, near_sem, far_sem,
):
    subjects = vi_ref.shape[0]
    depth = lab_hbm.shape[0]
    odd = odd_ref[0]
    facing = jnp.where(odd == 1, 0, depth - 1)
    sides = ((facing, vi_ref, near_ref, near_sem, 0), (depth - 1 - facing, vo_ref, far_ref, far_sem, 1))

    def fetch(s, z, buffer, sem):
        return pltpu.make_async_copy(old_hbm.at[s, :, pl.ds(z, 1)], buffer.at[s], sem.at[0, s])

    def store(s, z, buffer, sem):
        return pltpu.make_async_copy(buffer.at[s], out_hbm.at[s, :, pl.ds(z, 1)], sem.at[1, s])

    labels = [pltpu.make_async_copy(lab_hbm.at[z], lab_ref.at[side], lab_sem.at[side]) for z, *_, side in sides]
    for copy in labels:
        copy.start()
    for s in range(subjects):
        for z, _, buffer, sem, _ in sides:
            fetch(s, z, buffer, sem).start()
    for copy in labels:
        copy.wait()
    for s in range(subjects):
        for z, halo, buffer, sem, side in sides:
            fetch(s, z, buffer, sem).wait()
            rate = rate_at(lab_ref[side], stiff)
            for c in range(3):
                buffer[s, c, 0] = buffer[s, c, 0] + rate * halo[s, c, 0]
            store(s, z, buffer, sem).start()
    for s in range(subjects):
        for z, _, buffer, sem, _ in sides:
            store(s, z, buffer, sem).wait()


SMALL = pl.BlockSpec(memory_space=pltpu.SMEM)
FAR = pl.BlockSpec(memory_space=pltpu.HBM)
FREE = pl.BlockSpec(memory_space=pl.ANY)
NEAR = pl.BlockSpec(memory_space=pltpu.VMEM)
COPY = pltpu.SemaphoreType.DMA


def share_update(place, scale, template, parts):
    return pl.pallas_call(
        lambda *refs: share_kernel(refs[0], scale, *refs[1:]),
        out_shape=jax.ShapeDtypeStruct(parts.shape, jnp.float32),
        in_specs=[SMALL, FAR, NEAR],
        out_specs=NEAR,
        scratch_shapes=[pltpu.VMEM(template.shape[1:], jnp.float32), COPY(())],
        compiler_params=pltpu.CompilerParams(vmem_limit_bytes=8 * MIB),
        cost_estimate=pl.CostEstimate(flops=parts.size, bytes_accessed=2 * MIB, transcendentals=0),
        name="share_update",
    )(place, template, parts)


def moved(odd, cohort, gain, stiffness, template, t_inner, t_outer, labels, images, velocity):
    subjects = images.shape[0]
    depth, count, width = template.shape
    edge = jax.ShapeDtypeStruct((subjects, 3, 1, count, width), jnp.float32)
    whole = jax.ShapeDtypeStruct(velocity.shape, jnp.float32)
    return pl.pallas_call(
        move_kernel,
        out_shape=[jax.ShapeDtypeStruct(template.shape, jnp.float32), edge, edge, whole],
        in_specs=[SMALL] * 4 + [FAR] * 6,
        out_specs=[NEAR, FAR, FAR, FAR],
        scratch_shapes=[
            pltpu.VMEM((depth + 2, count, width), jnp.float32),
            pltpu.VMEM(labels.shape, labels.dtype),
            pltpu.VMEM(images.shape, images.dtype),
            pltpu.VMEM((subjects, 3, depth + 2, count, width), jnp.float32),
            pltpu.VMEM(velocity.shape, jnp.float32),
            pltpu.VMEM((3,) + template.shape, jnp.float32),
            pltpu.VMEM(template.shape, jnp.float32),
            COPY((3,)), COPY(()), COPY((subjects,)), COPY((subjects, 3)),
            COPY((subjects,)), COPY((subjects,)), COPY((subjects, 2)),
        ],
        compiler_params=pltpu.CompilerParams(vmem_limit_bytes=60 * MIB),
        cost_estimate=pl.CostEstimate(flops=8 * velocity.size, bytes_accessed=16 * MIB, transcendentals=0),
        name="moved",
    )(odd, cohort, gain, stiffness, template, t_inner, t_outer, labels, images, velocity)


def edges_added(odd, stiffness, labels, v_inner, v_outer, velocity):
    subjects = velocity.shape[0]
    count, width = labels.shape[1:]
    return pl.pallas_call(
        edge_kernel,
        out_shape=jax.ShapeDtypeStruct(velocity.shape, jnp.float32),
        in_specs=[SMALL] * 2 + [FAR, NEAR, NEAR, FAR],
        out_specs=FAR,
        scratch_shapes=[
            pltpu.VMEM((2, count, width), labels.dtype),
            pltpu.VMEM(v_inner.shape, jnp.float32),
            pltpu.VMEM(v_outer.shape, jnp.float32),
            COPY((2,)), COPY((2, subjects)), COPY((2, subjects)),
        ],
        input_output_aliases={5: 0},
        compiler_params=pltpu.CompilerParams(vmem_limit_bytes=50 * MIB),
        cost_estimate=pl.CostEstimate(flops=v_inner.size, bytes_accessed=6 * MIB, transcendentals=0),
        name="edges_added",
    )(odd, stiffness, labels, v_inner, v_outer, velocity)


def local(template, images, velocity, labels, stiffness, cohort, site_gain):
    depth = template.shape[0]
    slabs = lax.axis_size("slab")
    groups = lax.axis_size("grp")
    assert depth == groups and slabs % 2 == 0
    odd = lax.axis_index("slab") % 2
    place = lax.axis_index("grp").reshape(1)
    inside = [(i, i ^ 1) for i in range(slabs)]
    across = [(i, i + 1) for i in range(1, slabs - 1, 2)]
    across = across + [(target, source) for source, target in across]
    facing = jnp.where(odd == 1, 0, depth - 1)
    t_inner = lax.ppermute(lax.dynamic_slice_in_dim(template, facing, 1, 0), "slab", inside)
    t_outer = lax.ppermute(lax.dynamic_slice_in_dim(template, depth - 1 - facing, 1, 0), "slab", across)
    odd = odd.reshape(1)
    part, inner, outer, new_velocity = moved(
        odd, cohort, site_gain, stiffness, template, t_inner, t_outer, labels, images, velocity
    )
    v_inner = lax.ppermute(inner, "slab", inside)
    v_outer = lax.ppermute(outer, "slab", across)
    parts = lax.all_to_all(part, "grp", 0, 0, tiled=True)
    shares = share_update(place, template_step / (images.shape[0] * groups), template, parts)
    new_template = lax.all_to_all(shares, "grp", 0, 0, tiled=True)
    new_velocity = edges_added(odd, stiffness, labels, v_inner, v_outer, new_velocity)
    return (new_template, new_velocity)


def solution(mesh):
    placed = (
        P("slab", None, None),
        P("grp", "slab", None, None),
        P("grp", None, "slab", None, None),
        P("slab", None, None),
        P(),
        P("grp"),
        P(),
    )
    return jax.shard_map(
        local,
        mesh=mesh,
        in_specs=placed,
        out_specs=(P("slab", None, None), P("grp", None, "slab", None, None)),
        check_vma=False,
    )
```

```python
import functools

import jax
import jax.numpy as jnp
from jax import lax
from jax.experimental import pallas as pl
from jax.experimental.pallas import tpu as pltpu
from jax.sharding import PartitionSpec as P

velocity_step = 0.05
template_step = 0.5
ROWS = 16
MIB = 1 << 20


def beside_y(get_row, here, first, last, count, start):
    rows, width = here.shape
    at = lax.broadcasted_iota(jnp.int32, (rows, width), 0)
    zero = jnp.zeros((rows, width), jnp.float32)
    before = zero if first else jnp.broadcast_to(get_row(start - 1), (rows, width))
    after = zero if last else jnp.broadcast_to(get_row(start + rows), (rows, width))
    lower = jnp.where(at == 0, before, pltpu.roll(here, 1, 0))
    upper = jnp.where(at == rows - 1, after, pltpu.roll(here, rows - 1, 0))
    return lower, upper


def beside_x(here):
    rows, width = here.shape
    at = lax.broadcasted_iota(jnp.int32, (rows, width), 1)
    zero = jnp.zeros((rows, width), jnp.float32)
    lower = jnp.where(at == 0, zero, pltpu.roll(here, 1, 1))
    upper = jnp.where(at == width - 1, zero, pltpu.roll(here, width - 1, 1))
    return lower, upper


def fill_slopes(t_ref, s_ref, also=None):
    depth, count, width = s_ref.shape[1:]

    @pl.loop(0, depth)
    def _(z):
        for j in range(count // ROWS):
            start = j * ROWS
            rows = pl.ds(start, ROWS)
            here = t_ref[z + 1, rows, :]
            y_low, y_high = beside_y(
                lambda at: t_ref[z + 1, pl.ds(at, 1), :], here, j == 0, start + ROWS == count, count, start
            )
            x_low, x_high = beside_x(here)
            s_ref[0, z, rows, :] = 0.5 * (t_ref[z + 2, rows, :] - t_ref[z, rows, :])
            s_ref[1, z, rows, :] = 0.5 * (y_high - y_low)
            s_ref[2, z, rows, :] = 0.5 * (x_high - x_low)
            if also is not None:
                also(z, rows)


def template_copies(odd, t_hbm, ti_hbm, to_hbm, t_ref, sem):
    depth = t_hbm.shape[0]
    inner = jnp.where(odd == 1, 0, depth + 1)
    outer = depth + 1 - inner
    return [
        pltpu.make_async_copy(t_hbm, t_ref.at[pl.ds(1, depth)], sem.at[0]),
        pltpu.make_async_copy(ti_hbm, t_ref.at[pl.ds(inner, 1)], sem.at[1]),
        pltpu.make_async_copy(to_hbm, t_ref.at[pl.ds(outer, 1)], sem.at[2]),
    ]


def partial_kernel(
    odd_ref, cohort, gain, t_hbm, ti_hbm, to_hbm, im_hbm, v_hbm, sum_ref, inner_hbm, outer_hbm,
    t_ref, im_ref, v_ref, s_ref, t_sem, im_sem, v_sem, in_sem, out_sem,
):
    subjects, depth, count, width = im_ref.shape
    odd = odd_ref[0]
    template = template_copies(odd, t_hbm, ti_hbm, to_hbm, t_ref, t_sem)
    images = [pltpu.make_async_copy(im_hbm.at[s], im_ref.at[s], im_sem.at[s]) for s in range(subjects)]
    fields = [
        [pltpu.make_async_copy(v_hbm.at[s, c], v_ref.at[s, c], v_sem.at[s, c]) for c in range(3)]
        for s in range(subjects)
    ]
    facing = jnp.where(odd == 1, 0, depth - 1)
    inner = [
        pltpu.make_async_copy(v_ref.at[s, :, pl.ds(facing, 1)], inner_hbm.at[s], in_sem.at[s])
        for s in range(subjects)
    ]
    outer = [
        pltpu.make_async_copy(v_ref.at[s, :, pl.ds(depth - 1 - facing, 1)], outer_hbm.at[s], out_sem.at[s])
        for s in range(subjects)
    ]
    for copy in template:
        copy.start()
    for s in range(subjects):
        images[s].start()
        for copy in fields[s]:
            copy.start()
    for copy in template:
        copy.wait()
    fill_slopes(t_ref, s_ref)
    pair = 2 if subjects % 2 == 0 else 1
    for low in range(0, subjects, pair):
        members = range(low, low + pair)
        for s in members:
            images[s].wait()
            for copy in fields[s]:
                copy.wait()
            inner[s].start()
            outer[s].start()
        levels = [gain[cohort[s]] for s in members]

        @pl.loop(0, depth)
        def _(z):
            for j in range(count // ROWS):
                rows = pl.ds(j * ROWS, ROWS)
                value = float(pair) * t_ref[z + 1, rows, :]
                for s, level in zip(members, levels):
                    value = value - level * im_ref[s, z, rows, :].astype(jnp.float32)
                for c in range(3):
                    field = v_ref[low, c, z, rows, :]
                    for s in members[1:]:
                        field = field + v_ref[s, c, z, rows, :]
                    value = value + s_ref[c, z, rows, :] * field
                if low:
                    value = value + sum_ref[z, rows, :]
                sum_ref[z, rows, :] = value

    for copy in inner + outer:
        copy.wait()


def share_kernel(place, scale, t_hbm, parts_ref, _, out_ref, mark_ref, own_ref, sem):
    mark_ref[...] = jnp.zeros_like(mark_ref)
    groups, count, width = parts_ref.shape
    copy = pltpu.make_async_copy(t_hbm.at[place[0]], own_ref, sem)
    copy.start()
    copy.wait()
    for j in range(count // ROWS):
        rows = pl.ds(j * ROWS, ROWS)
        total = parts_ref[0, rows, :]
        for g in range(1, groups):
            total = total + parts_ref[g, rows, :]
        value = own_ref[rows, :] - scale * total
        for g in range(groups):
            out_ref[g, rows, :] = value


def rate_at(label, stiff):
    rate = jnp.full(label.shape, stiff[0], jnp.float32)
    for kind in range(1, stiff.shape[0]):
        rate = jnp.where(label == kind, stiff[kind], rate)
    return velocity_step * rate


def move_kernel(first, final, odd_ref, cohort, gain, stiff, t_hbm, ti_hbm, to_hbm, lab_hbm, im_hbm, v_hbm, *refs):
    if final:
        vi_ref, vo_ref, old_hbm, _, out_hbm, *refs = refs
    else:
        _, out_hbm, mark_ref, *refs = refs
        mark_ref[...] = jnp.zeros_like(mark_ref)
    t_ref, lab_ref, im_ref, v_ref, new_ref, s_ref, k_ref, t_sem, lab_sem, im_sem, v_sem, out_sem, *refs = refs
    subjects, depth, count, width = im_ref.shape
    odd = odd_ref[0]
    template = template_copies(odd, t_hbm, ti_hbm, to_hbm, t_ref, t_sem)
    template.append(pltpu.make_async_copy(lab_hbm, lab_ref, lab_sem))
    facing = jnp.where(odd == 1, 0, depth - 1)
    half = depth // 2

    def arrivals(s):
        copies = [pltpu.make_async_copy(im_hbm.at[first + s], im_ref.at[s], im_sem.at[s])]
        for c in range(3):
            copies.append(
                pltpu.make_async_copy(v_hbm.at[first + s, c], v_ref.at[s, c, pl.ds(1, depth)], v_sem.at[s, c])
            )
        return copies

    def departure(s, part):
        planes = pl.ds(part * half, half)
        return pltpu.make_async_copy(
            new_ref.at[s, :, planes], out_hbm.at[first + s, :, planes], out_sem.at[s, part]
        )

    for copy in template:
        copy.start()
    for s in range(subjects):
        for copy in arrivals(s):
            copy.start()
    if final:
        near_ref, far_ref, near_sem, far_sem = refs
        sides = ((facing, vi_ref, near_ref, near_sem), (depth - 1 - facing, vo_ref, far_ref, far_sem))

        def fetch(s, z, buffer, sem):
            return pltpu.make_async_copy(old_hbm.at[s, :, pl.ds(z, 1)], buffer.at[s], sem.at[0, s])

        def store(s, z, buffer, sem):
            return pltpu.make_async_copy(buffer.at[s], out_hbm.at[s, :, pl.ds(z, 1)], sem.at[1, s])

        for s in range(first):
            for z, _, buffer, sem in sides:
                fetch(s, z, buffer, sem).start()
    outside = jnp.zeros((count, width), jnp.float32)
    inner = jnp.where(odd == 1, 0, depth + 1)
    for s in range(subjects):
        for c in range(3):
            v_ref[s, c, inner] = vi_ref[first + s, c, 0] if final else outside
            v_ref[s, c, depth + 1 - inner] = vo_ref[first + s, c, 0] if final else outside
    for copy in template:
        copy.wait()

    def rate_of(z, rows):
        k_ref[z, rows, :] = rate_at(lab_ref[z, rows, :], stiff)

    fill_slopes(t_ref, s_ref, rate_of)
    if final:
        for s in range(first):
            for z, halo, buffer, sem in sides:
                fetch(s, z, buffer, sem).wait()
                for c in range(3):
                    buffer[s, c, 0] = buffer[s, c, 0] + k_ref[z] * halo[s, c, 0]
                store(s, z, buffer, sem).start()

    @pl.loop(0, subjects)
    def _(s):
        for copy in arrivals(s):
            copy.wait()
        level = gain[cohort[first + s]]

        def plane(z):
            for j in range(count // ROWS):
                start = j * ROWS
                rows = pl.ds(start, ROWS)
                field = [v_ref[s, c, z + 1, rows, :] for c in range(3)]
                slopes = [s_ref[c, z, rows, :] for c in range(3)]
                rate = k_ref[z, rows, :]
                value = t_ref[z + 1, rows, :] - level * im_ref[s, z, rows, :].astype(jnp.float32)
                for c in range(3):
                    value = value + slopes[c] * field[c]
                value = velocity_step * value
                for c in range(3):
                    here = field[c]
                    y_low, y_high = beside_y(
                        lambda at: v_ref[s, c, z + 1, pl.ds(at, 1), :], here,
                        j == 0, start + ROWS == count, count, start,
                    )
                    x_low, x_high = beside_x(here)
                    around = (v_ref[s, c, z, rows, :] + v_ref[s, c, z + 2, rows, :]) + (y_low + y_high)
                    around = around + (x_low + x_high)
                    new_ref[s, c, z, rows, :] = here + rate * (around - 6.0 * here) - value * slopes[c]

        for part in range(2):
            pl.loop(part * half, (part + 1) * half)(plane)
            departure(s, part).start()

    if final:
        for s in range(first):
            for z, _, buffer, sem in sides:
                store(s, z, buffer, sem).wait()

    @pl.loop(0, subjects)
    def _(s):
        for part in range(2):
            departure(s, part).wait()


SMALL = pl.BlockSpec(memory_space=pltpu.SMEM)
FAR = pl.BlockSpec(memory_space=pltpu.HBM)
FREE = pl.BlockSpec(memory_space=pl.ANY)
NEAR = pl.BlockSpec(memory_space=pltpu.VMEM)
COPY = pltpu.SemaphoreType.DMA
MARK = jax.ShapeDtypeStruct((8, 128), jnp.float32)


def partial_sums(odd, cohort, gain, template, t_inner, t_outer, images, velocity):
    subjects = images.shape[0]
    depth, count, width = template.shape
    edge = jax.ShapeDtypeStruct((subjects, 3, 1, count, width), jnp.float32)
    return pl.pallas_call(
        partial_kernel,
        out_shape=[jax.ShapeDtypeStruct(template.shape, jnp.float32), edge, edge],
        in_specs=[SMALL] * 3 + [FAR, FREE, FREE, FAR, FAR],
        out_specs=[NEAR, FAR, FAR],
        scratch_shapes=[
            pltpu.VMEM((depth + 2, count, width), jnp.float32),
            pltpu.VMEM(images.shape, images.dtype),
            pltpu.VMEM(velocity.shape, jnp.float32),
            pltpu.VMEM((3,) + template.shape, jnp.float32),
            COPY((3,)), COPY((subjects,)), COPY((subjects, 3)), COPY((subjects,)), COPY((subjects,)),
        ],
        compiler_params=pltpu.CompilerParams(vmem_limit_bytes=60 * MIB),
        cost_estimate=pl.CostEstimate(flops=4 * velocity.size, bytes_accessed=10 * MIB, transcendentals=0),
        name="partial_sums",
    )(odd, cohort, gain, template, t_inner, t_outer, images, velocity)


def share_update(place, scale, template, parts, after):
    return pl.pallas_call(
        lambda *refs: share_kernel(refs[0], scale, *refs[1:]),
        out_shape=[jax.ShapeDtypeStruct(parts.shape, jnp.float32), MARK],
        in_specs=[SMALL, FAR, NEAR, FAR],
        out_specs=[NEAR, NEAR],
        scratch_shapes=[pltpu.VMEM(template.shape[1:], jnp.float32), COPY(())],
        compiler_params=pltpu.CompilerParams(vmem_limit_bytes=8 * MIB),
        cost_estimate=pl.CostEstimate(flops=parts.size, bytes_accessed=2 * MIB, transcendentals=0),
        name="share_update",
    )(place, template, parts, after)


def moved(first, last, odd, cohort, gain, stiffness, template, t_inner, t_outer, labels, images, velocity, after, earlier=()):
    final = bool(earlier)
    subjects = last - first
    depth, count, width = template.shape
    edge = (first, 3, 1, count, width)
    extra = [pltpu.VMEM(edge, jnp.float32)] * 2 + [COPY((2, first))] * 2 if final else []
    return pl.pallas_call(
        functools.partial(move_kernel, first, final),
        out_shape=[jax.ShapeDtypeStruct(velocity.shape, jnp.float32)] + ([] if final else [MARK]),
        in_specs=[SMALL] * 4 + [FAR] * 6 + ([NEAR, NEAR, FAR] if final else []) + [FAR],
        out_specs=[FAR] if final else [FAR, NEAR],
        scratch_shapes=[
            pltpu.VMEM((depth + 2, count, width), jnp.float32),
            pltpu.VMEM(labels.shape, labels.dtype),
            pltpu.VMEM((subjects,) + images.shape[1:], images.dtype),
            pltpu.VMEM((subjects, 3, depth + 2, count, width), jnp.float32),
            pltpu.VMEM((subjects,) + velocity.shape[1:], jnp.float32),
            pltpu.VMEM((3,) + template.shape, jnp.float32),
            pltpu.VMEM(template.shape, jnp.float32),
            COPY((3,)), COPY(()), COPY((subjects,)), COPY((subjects, 3)), COPY((subjects, 2)),
        ] + extra,
        input_output_aliases={12: 0} if final else {},
        compiler_params=pltpu.CompilerParams(vmem_limit_bytes=(50 if final else 60) * MIB),
        cost_estimate=pl.CostEstimate(flops=4 * velocity.size, bytes_accessed=8 * MIB, transcendentals=0),
        name="moved_last" if final else "moved_first",
    )(odd, cohort, gain, stiffness, template, t_inner, t_outer, labels, images, velocity, *earlier, after)


def local(template, images, velocity, labels, stiffness, cohort, site_gain):
    depth = template.shape[0]
    slabs = lax.axis_size("slab")
    groups = lax.axis_size("grp")
    assert depth == groups and slabs % 2 == 0
    odd = lax.axis_index("slab") % 2
    place = lax.axis_index("grp").reshape(1)
    inside = [(i, i ^ 1) for i in range(slabs)]
    across = [(i, i + 1) for i in range(1, slabs - 1, 2)]
    across = across + [(target, source) for source, target in across]
    facing = jnp.where(odd == 1, 0, depth - 1)
    t_inner = lax.ppermute(lax.dynamic_slice_in_dim(template, facing, 1, 0), "slab", inside)
    t_outer = lax.ppermute(lax.dynamic_slice_in_dim(template, depth - 1 - facing, 1, 0), "slab", across)
    odd = odd.reshape(1)
    part, inner, outer = partial_sums(odd, cohort, site_gain, template, t_inner, t_outer, images, velocity)
    v_inner = lax.ppermute(inner, "slab", inside)
    v_outer = lax.ppermute(outer, "slab", across)
    parts = lax.all_to_all(part, "grp", 0, 0, tiled=True)
    subjects = images.shape[0]
    split = subjects // 2
    shared = (odd, cohort, site_gain, stiffness, template, t_inner, t_outer, labels, images, velocity)
    begun, first_done = moved(0, split, *shared, part)
    shares, shares_done = share_update(place, template_step / (subjects * groups), template, parts, first_done)
    new_template = lax.all_to_all(shares, "grp", 0, 0, tiled=True)
    (new_velocity,) = moved(split, subjects, *shared, shares_done, (v_inner, v_outer, begun))
    return (new_template, new_velocity)


def solution(mesh):
    placed = (
        P("slab", None, None),
        P("grp", "slab", None, None),
        P("grp", None, "slab", None, None),
        P("slab", None, None),
        P(),
        P("grp"),
        P(),
    )
    return jax.shard_map(
        local,
        mesh=mesh,
        in_specs=placed,
        out_specs=(P("slab", None, None), P("grp", None, "slab", None, None)),
        check_vma=False,
    )
```

```python
import jax
import jax.numpy as jnp
from jax import lax
from jax.experimental import pallas as pl
from jax.experimental.pallas import tpu as pltpu
from jax.sharding import PartitionSpec as P

velocity_step = 0.05
template_step = 0.5
ROWS = 16
AHEAD = 2
MIB = 1 << 20


def beside_y(get_row, here, first, last, count, start):
    rows, width = here.shape
    at = lax.broadcasted_iota(jnp.int32, (rows, width), 0)
    zero = jnp.zeros((rows, width), jnp.float32)
    before = zero if first else jnp.broadcast_to(get_row(start - 1), (rows, width))
    after = zero if last else jnp.broadcast_to(get_row(start + rows), (rows, width))
    lower = jnp.where(at == 0, before, pltpu.roll(here, 1, 0))
    upper = jnp.where(at == rows - 1, after, pltpu.roll(here, rows - 1, 0))
    return lower, upper


def beside_x(here):
    rows, width = here.shape
    at = lax.broadcasted_iota(jnp.int32, (rows, width), 1)
    zero = jnp.zeros((rows, width), jnp.float32)
    lower = jnp.where(at == 0, zero, pltpu.roll(here, 1, 1))
    upper = jnp.where(at == width - 1, zero, pltpu.roll(here, width - 1, 1))
    return lower, upper


def fill_slopes(t_ref, s_ref, also=None):
    depth, count, width = s_ref.shape[1:]

    @pl.loop(0, depth)
    def _(z):
        for j in range(count // ROWS):
            start = j * ROWS
            rows = pl.ds(start, ROWS)
            here = t_ref[z + 1, rows, :]
            y_low, y_high = beside_y(
                lambda at: t_ref[z + 1, pl.ds(at, 1), :], here, j == 0, start + ROWS == count, count, start
            )
            x_low, x_high = beside_x(here)
            s_ref[0, z, rows, :] = 0.5 * (t_ref[z + 2, rows, :] - t_ref[z, rows, :])
            s_ref[1, z, rows, :] = 0.5 * (y_high - y_low)
            s_ref[2, z, rows, :] = 0.5 * (x_high - x_low)
            if also is not None:
                also(z, rows)


def template_copies(odd, t_hbm, ti_hbm, to_hbm, t_ref, sem):
    depth = t_hbm.shape[0]
    inner = jnp.where(odd == 1, 0, depth + 1)
    outer = depth + 1 - inner
    return [
        pltpu.make_async_copy(t_hbm, t_ref.at[pl.ds(1, depth)], sem.at[0]),
        pltpu.make_async_copy(ti_hbm, t_ref.at[pl.ds(inner, 1)], sem.at[1]),
        pltpu.make_async_copy(to_hbm, t_ref.at[pl.ds(outer, 1)], sem.at[2]),
    ]


def partial_kernel(
    odd_ref, cohort, gain, t_hbm, ti_hbm, to_hbm, im_hbm, v_hbm, sum_ref, inner_hbm, outer_hbm,
    t_ref, im_ref, v_ref, s_ref, t_sem, im_sem, v_sem, in_sem, out_sem,
):
    subjects, depth, count, width = im_ref.shape
    odd = odd_ref[0]
    template = template_copies(odd, t_hbm, ti_hbm, to_hbm, t_ref, t_sem)
    images = [pltpu.make_async_copy(im_hbm.at[s], im_ref.at[s], im_sem.at[s]) for s in range(subjects)]
    fields = [
        [pltpu.make_async_copy(v_hbm.at[s, c], v_ref.at[s, c], v_sem.at[s, c]) for c in range(3)]
        for s in range(subjects)
    ]
    facing = jnp.where(odd == 1, 0, depth - 1)
    inner = [
        pltpu.make_async_copy(v_ref.at[s, :, pl.ds(facing, 1)], inner_hbm.at[s], in_sem.at[s])
        for s in range(subjects)
    ]
    outer = [
        pltpu.make_async_copy(v_ref.at[s, :, pl.ds(depth - 1 - facing, 1)], outer_hbm.at[s], out_sem.at[s])
        for s in range(subjects)
    ]
    for copy in template:
        copy.start()
    pair = 2 if subjects % 2 == 0 else 1

    def begin(members):
        for s in members:
            images[s].start()
            for copy in fields[s]:
                copy.start()

    begin(range(pair))
    for copy in template:
        copy.wait()
    begin(range(pair, subjects))
    fill_slopes(t_ref, s_ref)
    for low in range(0, subjects, pair):
        members = range(low, low + pair)
        for s in members:
            images[s].wait()
            for copy in fields[s]:
                copy.wait()
            inner[s].start()
            outer[s].start()
        levels = [gain[cohort[s]] for s in members]

        @pl.loop(0, depth)
        def _(z):
            for j in range(count // ROWS):
                rows = pl.ds(j * ROWS, ROWS)
                value = float(pair) * t_ref[z + 1, rows, :]
                for s, level in zip(members, levels):
                    value = value - level * im_ref[s, z, rows, :].astype(jnp.float32)
                for c in range(3):
                    field = v_ref[low, c, z, rows, :]
                    for s in members[1:]:
                        field = field + v_ref[s, c, z, rows, :]
                    value = value + s_ref[c, z, rows, :] * field
                if low:
                    value = value + sum_ref[z, rows, :]
                sum_ref[z, rows, :] = value

    for copy in inner + outer:
        copy.wait()


def share_kernel(place, scale, t_hbm, parts_ref, out_ref, own_ref, sem):
    groups, count, width = parts_ref.shape
    copy = pltpu.make_async_copy(t_hbm.at[place[0]], own_ref, sem)
    copy.start()
    copy.wait()
    for j in range(count // ROWS):
        rows = pl.ds(j * ROWS, ROWS)
        total = parts_ref[0, rows, :]
        for g in range(1, groups):
            total = total + parts_ref[g, rows, :]
        value = own_ref[rows, :] - scale * total
        for g in range(groups):
            out_ref[g, rows, :] = value


def move_kernel(
    odd_ref, cohort, gain, stiff, t_hbm, ti_hbm, to_hbm, lab_hbm, im_hbm, v_hbm, vi_hbm, vo_hbm, out_hbm,
    t_ref, lab_ref, im_ref, v_ref, new_ref, s_ref, k_ref,
    t_sem, lab_sem, im_sem, v_sem, vi_sem, vo_sem, out_sem,
):
    subjects, depth, count, width = im_ref.shape
    odd = odd_ref[0]
    template = template_copies(odd, t_hbm, ti_hbm, to_hbm, t_ref, t_sem)
    template.append(pltpu.make_async_copy(lab_hbm, lab_ref, lab_sem))
    inner = jnp.where(odd == 1, 0, depth + 1)
    half = depth // 2

    def arrivals(s):
        copies = [pltpu.make_async_copy(im_hbm.at[s], im_ref.at[s], im_sem.at[s])]
        for c in range(3):
            copies.append(
                pltpu.make_async_copy(v_hbm.at[s, c], v_ref.at[s, c, pl.ds(1, depth)], v_sem.at[s, c])
            )
        copies.append(pltpu.make_async_copy(vi_hbm.at[s], v_ref.at[s, :, pl.ds(inner, 1)], vi_sem.at[s]))
        copies.append(
            pltpu.make_async_copy(vo_hbm.at[s], v_ref.at[s, :, pl.ds(depth + 1 - inner, 1)], vo_sem.at[s])
        )
        return copies

    def departure(s, part):
        planes = pl.ds(part * half, half)
        return pltpu.make_async_copy(new_ref.at[s, :, planes], out_hbm.at[s, :, planes], out_sem.at[s, part])

    for copy in template:
        copy.start()
    ahead = min(AHEAD, subjects)
    for s in range(ahead):
        for copy in arrivals(s):
            copy.start()
    for copy in template:
        copy.wait()

    def rate_of(z, rows):
        label = lab_ref[z, rows, :]
        rate = jnp.full(label.shape, stiff[0], jnp.float32)
        for kind in range(1, stiff.shape[0]):
            rate = jnp.where(label == kind, stiff[kind], rate)
        k_ref[z, rows, :] = velocity_step * rate

    fill_slopes(t_ref, s_ref, rate_of)

    @pl.loop(0, subjects)
    def _(s):
        for copy in arrivals(s):
            copy.wait()

        @pl.when(s + ahead < subjects)
        def _():
            for copy in arrivals(s + ahead):
                copy.start()

        level = gain[cohort[s]]

        def plane(z):
            for j in range(count // ROWS):
                start = j * ROWS
                rows = pl.ds(start, ROWS)
                field = [v_ref[s, c, z + 1, rows, :] for c in range(3)]
                slopes = [s_ref[c, z, rows, :] for c in range(3)]
                rate = k_ref[z, rows, :]
                value = t_ref[z + 1, rows, :] - level * im_ref[s, z, rows, :].astype(jnp.float32)
                for c in range(3):
                    value = value + slopes[c] * field[c]
                value = velocity_step * value
                for c in range(3):
                    here = field[c]
                    y_low, y_high = beside_y(
                        lambda at: v_ref[s, c, z + 1, pl.ds(at, 1), :], here,
                        j == 0, start + ROWS == count, count, start,
                    )
                    x_low, x_high = beside_x(here)
                    around = (v_ref[s, c, z, rows, :] + v_ref[s, c, z + 2, rows, :]) + (y_low + y_high)
                    around = around + (x_low + x_high)
                    new_ref[s, c, z, rows, :] = here + rate * (around - 6.0 * here) - value * slopes[c]

        for part in range(2):
            pl.loop(part * half, (part + 1) * half)(plane)
            departure(s, part).start()

    @pl.loop(0, subjects)
    def _(s):
        for part in range(2):
            departure(s, part).wait()


SMALL = pl.BlockSpec(memory_space=pltpu.SMEM)
FAR = pl.BlockSpec(memory_space=pltpu.HBM)
FREE = pl.BlockSpec(memory_space=pl.ANY)
NEAR = pl.BlockSpec(memory_space=pltpu.VMEM)
COPY = pltpu.SemaphoreType.DMA


def partial_sums(odd, cohort, gain, template, t_inner, t_outer, images, velocity):
    subjects = images.shape[0]
    depth, count, width = template.shape
    edge = jax.ShapeDtypeStruct((subjects, 3, 1, count, width), jnp.float32)
    return pl.pallas_call(
        partial_kernel,
        out_shape=[jax.ShapeDtypeStruct(template.shape, jnp.float32), edge, edge],
        in_specs=[SMALL] * 3 + [FAR, FREE, FREE, FAR, FAR],
        out_specs=[NEAR, FAR, FAR],
        scratch_shapes=[
            pltpu.VMEM((depth + 2, count, width), jnp.float32),
            pltpu.VMEM(images.shape, images.dtype),
            pltpu.VMEM(velocity.shape, jnp.float32),
            pltpu.VMEM((3,) + template.shape, jnp.float32),
            COPY((3,)), COPY((subjects,)), COPY((subjects, 3)), COPY((subjects,)), COPY((subjects,)),
        ],
        compiler_params=pltpu.CompilerParams(vmem_limit_bytes=60 * MIB),
        cost_estimate=pl.CostEstimate(flops=4 * velocity.size, bytes_accessed=10 * MIB, transcendentals=0),
        name="partial_sums",
    )(odd, cohort, gain, template, t_inner, t_outer, images, velocity)


def share_update(place, scale, template, parts):
    return pl.pallas_call(
        lambda *refs: share_kernel(refs[0], scale, *refs[1:]),
        out_shape=jax.ShapeDtypeStruct(parts.shape, jnp.float32),
        in_specs=[SMALL, FAR, NEAR],
        out_specs=NEAR,
        scratch_shapes=[pltpu.VMEM(template.shape[1:], jnp.float32), COPY(())],
        compiler_params=pltpu.CompilerParams(vmem_limit_bytes=8 * MIB),
        cost_estimate=pl.CostEstimate(flops=parts.size, bytes_accessed=2 * MIB, transcendentals=0),
        name="share_update",
    )(place, template, parts)


def moved(odd, cohort, gain, stiffness, template, t_inner, t_outer, labels, images, velocity, v_inner, v_outer):
    subjects = images.shape[0]
    depth, count, width = template.shape
    return pl.pallas_call(
        move_kernel,
        out_shape=jax.ShapeDtypeStruct(velocity.shape, jnp.float32),
        in_specs=[SMALL] * 4 + [FAR, FREE, FREE, FAR, FAR, FAR, FREE, FREE],
        out_specs=FAR,
        scratch_shapes=[
            pltpu.VMEM((depth + 2, count, width), jnp.float32),
            pltpu.VMEM(labels.shape, labels.dtype),
            pltpu.VMEM(images.shape, images.dtype),
            pltpu.VMEM((subjects, 3, depth + 2, count, width), jnp.float32),
            pltpu.VMEM(velocity.shape, jnp.float32),
            pltpu.VMEM((3,) + template.shape, jnp.float32),
            pltpu.VMEM(template.shape, jnp.float32),
            COPY((3,)), COPY(()), COPY((subjects,)), COPY((subjects, 3)),
            COPY((subjects,)), COPY((subjects,)), COPY((subjects, 2)),
        ],
        compiler_params=pltpu.CompilerParams(vmem_limit_bytes=60 * MIB),
        cost_estimate=pl.CostEstimate(flops=8 * velocity.size, bytes_accessed=16 * MIB, transcendentals=0),
        name="moved",
    )(odd, cohort, gain, stiffness, template, t_inner, t_outer, labels, images, velocity, v_inner, v_outer)


def local(template, images, velocity, labels, stiffness, cohort, site_gain):
    depth = template.shape[0]
    slabs = lax.axis_size("slab")
    groups = lax.axis_size("grp")
    assert depth == groups and slabs % 2 == 0
    odd = lax.axis_index("slab") % 2
    place = lax.axis_index("grp").reshape(1)
    inside = [(i, i ^ 1) for i in range(slabs)]
    across = [(i, i + 1) for i in range(1, slabs - 1, 2)]
    across = across + [(target, source) for source, target in across]
    facing = jnp.where(odd == 1, 0, depth - 1)
    t_inner = lax.ppermute(lax.dynamic_slice_in_dim(template, facing, 1, 0), "slab", inside)
    t_outer = lax.ppermute(lax.dynamic_slice_in_dim(template, depth - 1 - facing, 1, 0), "slab", across)
    odd = odd.reshape(1)
    part, inner, outer = partial_sums(odd, cohort, site_gain, template, t_inner, t_outer, images, velocity)
    v_inner = lax.ppermute(inner, "slab", inside)
    v_outer = lax.ppermute(outer, "slab", across)
    parts = lax.all_to_all(part, "grp", 0, 0, tiled=True)
    shares = share_update(place, template_step / (images.shape[0] * groups), template, parts)
    new_template = lax.all_to_all(shares, "grp", 0, 0, tiled=True)
    new_velocity = moved(
        odd, cohort, site_gain, stiffness, template, t_inner, t_outer, labels, images, velocity, v_inner, v_outer
    )
    return (new_template, new_velocity)


def solution(mesh):
    placed = (
        P("slab", None, None),
        P("grp", "slab", None, None),
        P("grp", None, "slab", None, None),
        P("slab", None, None),
        P(),
        P("grp"),
        P(),
    )
    return jax.shard_map(
        local,
        mesh=mesh,
        in_specs=placed,
        out_specs=(P("slab", None, None), P("grp", None, "slab", None, None)),
        check_vma=False,
    )
```

```python
import jax
import jax.numpy as jnp
from jax import lax
from jax.experimental import pallas as pl
from jax.experimental.pallas import tpu as pltpu
from jax.sharding import PartitionSpec as P

velocity_step = 0.05
template_step = 0.5
ROWS = 16
AHEAD = 2
MIB = 1 << 20


def beside_y(get_row, here, first, last, count, start):
    rows, width = here.shape
    at = lax.broadcasted_iota(jnp.int32, (rows, width), 0)
    zero = jnp.zeros((rows, width), jnp.float32)
    before = zero if first else jnp.broadcast_to(get_row(start - 1), (rows, width))
    after = zero if last else jnp.broadcast_to(get_row(start + rows), (rows, width))
    lower = jnp.where(at == 0, before, pltpu.roll(here, 1, 0))
    upper = jnp.where(at == rows - 1, after, pltpu.roll(here, rows - 1, 0))
    return lower, upper


def beside_x(here):
    rows, width = here.shape
    at = lax.broadcasted_iota(jnp.int32, (rows, width), 1)
    zero = jnp.zeros((rows, width), jnp.float32)
    lower = jnp.where(at == 0, zero, pltpu.roll(here, 1, 1))
    upper = jnp.where(at == width - 1, zero, pltpu.roll(here, width - 1, 1))
    return lower, upper


def fill_slopes(t_ref, s_ref, also=None):
    depth, count, width = s_ref.shape[1:]

    @pl.loop(0, depth)
    def _(z):
        for j in range(count // ROWS):
            start = j * ROWS
            rows = pl.ds(start, ROWS)
            here = t_ref[z + 1, rows, :]
            y_low, y_high = beside_y(
                lambda at: t_ref[z + 1, pl.ds(at, 1), :], here, j == 0, start + ROWS == count, count, start
            )
            x_low, x_high = beside_x(here)
            s_ref[0, z, rows, :] = 0.5 * (t_ref[z + 2, rows, :] - t_ref[z, rows, :])
            s_ref[1, z, rows, :] = 0.5 * (y_high - y_low)
            s_ref[2, z, rows, :] = 0.5 * (x_high - x_low)
            if also is not None:
                also(z, rows)


def template_copies(odd, t_hbm, ti_hbm, to_hbm, t_ref, sem):
    depth = t_hbm.shape[0]
    inner = jnp.where(odd == 1, 0, depth + 1)
    outer = depth + 1 - inner
    return [
        pltpu.make_async_copy(t_hbm, t_ref.at[pl.ds(1, depth)], sem.at[0]),
        pltpu.make_async_copy(ti_hbm, t_ref.at[pl.ds(inner, 1)], sem.at[1]),
        pltpu.make_async_copy(to_hbm, t_ref.at[pl.ds(outer, 1)], sem.at[2]),
    ]


def share_kernel(place, scale, t_hbm, parts_ref, out_ref, own_ref, sem):
    groups, count, width = parts_ref.shape
    copy = pltpu.make_async_copy(t_hbm.at[place[0]], own_ref, sem)
    copy.start()
    copy.wait()
    for j in range(count // ROWS):
        rows = pl.ds(j * ROWS, ROWS)
        total = parts_ref[0, rows, :]
        for g in range(1, groups):
            total = total + parts_ref[g, rows, :]
        value = own_ref[rows, :] - scale * total
        for g in range(groups):
            out_ref[g, rows, :] = value


def move_kernel(
    odd_ref, cohort, gain, stiff, t_hbm, ti_hbm, to_hbm, lab_hbm, im_hbm, v_hbm,
    sum_ref, inner_hbm, outer_hbm, out_hbm,
    t_ref, lab_ref, im_ref, v_ref, new_ref, s_ref, k_ref,
    t_sem, lab_sem, im_sem, v_sem, in_sem, far_sem, out_sem,
):
    subjects, depth, count, width = im_ref.shape
    odd = odd_ref[0]
    template = template_copies(odd, t_hbm, ti_hbm, to_hbm, t_ref, t_sem)
    template.append(pltpu.make_async_copy(lab_hbm, lab_ref, lab_sem))
    facing = jnp.where(odd == 1, 0, depth - 1)
    half = depth // 2

    def arrivals(s):
        copies = [pltpu.make_async_copy(im_hbm.at[s], im_ref.at[s], im_sem.at[s])]
        for c in range(3):
            copies.append(
                pltpu.make_async_copy(v_hbm.at[s, c], v_ref.at[s, c, pl.ds(1, depth)], v_sem.at[s, c])
            )
        return copies

    def edges(s):
        return [
            pltpu.make_async_copy(v_ref.at[s, :, pl.ds(1 + facing, 1)], inner_hbm.at[s], in_sem.at[s]),
            pltpu.make_async_copy(v_ref.at[s, :, pl.ds(depth - facing, 1)], outer_hbm.at[s], far_sem.at[s]),
        ]

    def departure(s, part):
        planes = pl.ds(part * half, half)
        return pltpu.make_async_copy(new_ref.at[s, :, planes], out_hbm.at[s, :, planes], out_sem.at[s, part])

    for copy in template:
        copy.start()
    ahead = min(AHEAD, subjects)
    for s in range(ahead):
        for copy in arrivals(s):
            copy.start()
    sum_ref[...] = jnp.zeros_like(sum_ref)
    outside = jnp.zeros((count, width), jnp.float32)

    @pl.loop(0, subjects)
    def _(s):
        for c in range(3):
            v_ref[s, c, 0] = outside
            v_ref[s, c, depth + 1] = outside

    for copy in template:
        copy.wait()

    def rate_of(z, rows):
        k_ref[z, rows, :] = rate_at(lab_ref[z, rows, :], stiff)

    fill_slopes(t_ref, s_ref, rate_of)

    @pl.loop(0, subjects)
    def _(s):
        for copy in arrivals(s):
            copy.wait()
        for copy in edges(s):
            copy.start()

        @pl.when(s + ahead < subjects)
        def _():
            for copy in arrivals(s + ahead):
                copy.start()

        level = gain[cohort[s]]

        def plane(z):
            for j in range(count // ROWS):
                start = j * ROWS
                rows = pl.ds(start, ROWS)
                field = [v_ref[s, c, z + 1, rows, :] for c in range(3)]
                slopes = [s_ref[c, z, rows, :] for c in range(3)]
                rate = k_ref[z, rows, :]
                value = t_ref[z + 1, rows, :] - level * im_ref[s, z, rows, :].astype(jnp.float32)
                for c in range(3):
                    value = value + slopes[c] * field[c]
                sum_ref[z, rows, :] = sum_ref[z, rows, :] + value
                value = velocity_step * value
                for c in range(3):
                    here = field[c]
                    y_low, y_high = beside_y(
                        lambda at: v_ref[s, c, z + 1, pl.ds(at, 1), :], here,
                        j == 0, start + ROWS == count, count, start,
                    )
                    x_low, x_high = beside_x(here)
                    around = (v_ref[s, c, z, rows, :] + v_ref[s, c, z + 2, rows, :]) + (y_low + y_high)
                    around = around + (x_low + x_high)
                    new_ref[s, c, z, rows, :] = here + rate * (around - 6.0 * here) - value * slopes[c]

        for part in range(2):
            pl.loop(part * half, (part + 1) * half)(plane)
            departure(s, part).start()

    @pl.loop(0, subjects)
    def _(s):
        for copy in edges(s):
            copy.wait()
        for part in range(2):
            departure(s, part).wait()


def rate_at(label, stiff):
    rate = jnp.full(label.shape, stiff[0], jnp.float32)
    for kind in range(1, stiff.shape[0]):
        rate = jnp.where(label == kind, stiff[kind], rate)
    return velocity_step * rate


def edge_kernel(
    odd_ref, stiff, lab_hbm, vi_ref, vo_ref, old_hbm, out_hbm, lab_ref, near_ref, far_ref,
    lab_sem, near_sem, far_sem,
):
    subjects = vi_ref.shape[0]
    depth = lab_hbm.shape[0]
    odd = odd_ref[0]
    facing = jnp.where(odd == 1, 0, depth - 1)
    sides = ((facing, vi_ref, near_ref, near_sem, 0), (depth - 1 - facing, vo_ref, far_ref, far_sem, 1))

    def fetch(s, z, buffer, sem):
        return pltpu.make_async_copy(old_hbm.at[s, :, pl.ds(z, 1)], buffer.at[s], sem.at[0, s])

    def store(s, z, buffer, sem):
        return pltpu.make_async_copy(buffer.at[s], out_hbm.at[s, :, pl.ds(z, 1)], sem.at[1, s])

    labels = [pltpu.make_async_copy(lab_hbm.at[z], lab_ref.at[side], lab_sem.at[side]) for z, *_, side in sides]
    for copy in labels:
        copy.start()
    for s in range(subjects):
        for z, _, buffer, sem, _ in sides:
            fetch(s, z, buffer, sem).start()
    for copy in labels:
        copy.wait()
    for s in range(subjects):
        for z, halo, buffer, sem, side in sides:
            fetch(s, z, buffer, sem).wait()
            rate = rate_at(lab_ref[side], stiff)
            for c in range(3):
                buffer[s, c, 0] = buffer[s, c, 0] + rate * halo[s, c, 0]
            store(s, z, buffer, sem).start()
    for s in range(subjects):
        for z, _, buffer, sem, _ in sides:
            store(s, z, buffer, sem).wait()


SMALL = pl.BlockSpec(memory_space=pltpu.SMEM)
FAR = pl.BlockSpec(memory_space=pltpu.HBM)
FREE = pl.BlockSpec(memory_space=pl.ANY)
NEAR = pl.BlockSpec(memory_space=pltpu.VMEM)
COPY = pltpu.SemaphoreType.DMA


def share_update(place, scale, template, parts):
    return pl.pallas_call(
        lambda *refs: share_kernel(refs[0], scale, *refs[1:]),
        out_shape=jax.ShapeDtypeStruct(parts.shape, jnp.float32),
        in_specs=[SMALL, FAR, NEAR],
        out_specs=NEAR,
        scratch_shapes=[pltpu.VMEM(template.shape[1:], jnp.float32), COPY(())],
        compiler_params=pltpu.CompilerParams(vmem_limit_bytes=8 * MIB),
        cost_estimate=pl.CostEstimate(flops=parts.size, bytes_accessed=2 * MIB, transcendentals=0),
        name="share_update",
    )(place, template, parts)


def moved(odd, cohort, gain, stiffness, template, t_inner, t_outer, labels, images, velocity):
    subjects = images.shape[0]
    depth, count, width = template.shape
    edge = jax.ShapeDtypeStruct((subjects, 3, 1, count, width), jnp.float32)
    whole = jax.ShapeDtypeStruct(velocity.shape, jnp.float32)
    return pl.pallas_call(
        move_kernel,
        out_shape=[jax.ShapeDtypeStruct(template.shape, jnp.float32), edge, edge, whole],
        in_specs=[SMALL] * 4 + [FAR] * 6,
        out_specs=[NEAR, FAR, FAR, FAR],
        scratch_shapes=[
            pltpu.VMEM((depth + 2, count, width), jnp.float32),
            pltpu.VMEM(labels.shape, labels.dtype),
            pltpu.VMEM(images.shape, images.dtype),
            pltpu.VMEM((subjects, 3, depth + 2, count, width), jnp.float32),
            pltpu.VMEM(velocity.shape, jnp.float32),
            pltpu.VMEM((3,) + template.shape, jnp.float32),
            pltpu.VMEM(template.shape, jnp.float32),
            COPY((3,)), COPY(()), COPY((subjects,)), COPY((subjects, 3)),
            COPY((subjects,)), COPY((subjects,)), COPY((subjects, 2)),
        ],
        compiler_params=pltpu.CompilerParams(vmem_limit_bytes=60 * MIB),
        cost_estimate=pl.CostEstimate(flops=8 * velocity.size, bytes_accessed=16 * MIB, transcendentals=0),
        name="moved",
    )(odd, cohort, gain, stiffness, template, t_inner, t_outer, labels, images, velocity)


def edges_added(odd, stiffness, labels, v_inner, v_outer, velocity):
    subjects = velocity.shape[0]
    count, width = labels.shape[1:]
    return pl.pallas_call(
        edge_kernel,
        out_shape=jax.ShapeDtypeStruct(velocity.shape, jnp.float32),
        in_specs=[SMALL] * 2 + [FAR, NEAR, NEAR, FAR],
        out_specs=FAR,
        scratch_shapes=[
            pltpu.VMEM((2, count, width), labels.dtype),
            pltpu.VMEM(v_inner.shape, jnp.float32),
            pltpu.VMEM(v_outer.shape, jnp.float32),
            COPY((2,)), COPY((2, subjects)), COPY((2, subjects)),
        ],
        input_output_aliases={5: 0},
        compiler_params=pltpu.CompilerParams(vmem_limit_bytes=50 * MIB),
        cost_estimate=pl.CostEstimate(flops=v_inner.size, bytes_accessed=6 * MIB, transcendentals=0),
        name="edges_added",
    )(odd, stiffness, labels, v_inner, v_outer, velocity)


def local(template, images, velocity, labels, stiffness, cohort, site_gain):
    depth = template.shape[0]
    slabs = lax.axis_size("slab")
    groups = lax.axis_size("grp")
    assert depth == groups and slabs % 2 == 0
    odd = lax.axis_index("slab") % 2
    place = lax.axis_index("grp").reshape(1)
    inside = [(i, i ^ 1) for i in range(slabs)]
    across = [(i, i + 1) for i in range(1, slabs - 1, 2)]
    across = across + [(target, source) for source, target in across]
    facing = jnp.where(odd == 1, 0, depth - 1)
    t_inner = lax.ppermute(lax.dynamic_slice_in_dim(template, facing, 1, 0), "slab", inside)
    t_outer = lax.ppermute(lax.dynamic_slice_in_dim(template, depth - 1 - facing, 1, 0), "slab", across)
    odd = odd.reshape(1)
    part, inner, outer, new_velocity = moved(
        odd, cohort, site_gain, stiffness, template, t_inner, t_outer, labels, images, velocity
    )
    v_inner = lax.ppermute(inner, "slab", inside)
    v_outer = lax.ppermute(outer, "slab", across)
    parts = lax.all_to_all(part, "grp", 0, 0, tiled=True)
    shares = share_update(place, template_step / (images.shape[0] * groups), template, parts)
    new_template = lax.all_to_all(shares, "grp", 0, 0, tiled=True)
    new_velocity = edges_added(odd, stiffness, labels, v_inner, v_outer, new_velocity)
    return (new_template, new_velocity)


def solution(mesh):
    placed = (
        P("slab", None, None),
        P("grp", "slab", None, None),
        P("grp", None, "slab", None, None),
        P("slab", None, None),
        P(),
        P("grp"),
        P(),
    )
    return jax.shard_map(
        local,
        mesh=mesh,
        in_specs=placed,
        out_specs=(P("slab", None, None), P("grp", None, "slab", None, None)),
        check_vma=False,
    )
```

```python
import jax
import jax.numpy as jnp
from jax import lax
from jax.experimental import pallas as pl
from jax.experimental.pallas import tpu as pltpu
from jax.sharding import PartitionSpec as P

velocity_step = 0.05
template_step = 0.5
ROWS = 16
AHEAD = 2
MIB = 1 << 20


def beside_y(get_row, here, first, last, count, start):
    rows, width = here.shape
    at = lax.broadcasted_iota(jnp.int32, (rows, width), 0)
    zero = jnp.zeros((rows, width), jnp.float32)
    before = zero if first else jnp.broadcast_to(get_row(start - 1), (rows, width))
    after = zero if last else jnp.broadcast_to(get_row(start + rows), (rows, width))
    lower = jnp.where(at == 0, before, pltpu.roll(here, 1, 0))
    upper = jnp.where(at == rows - 1, after, pltpu.roll(here, rows - 1, 0))
    return lower, upper


def beside_x(here):
    rows, width = here.shape
    at = lax.broadcasted_iota(jnp.int32, (rows, width), 1)
    zero = jnp.zeros((rows, width), jnp.float32)
    lower = jnp.where(at == 0, zero, pltpu.roll(here, 1, 1))
    upper = jnp.where(at == width - 1, zero, pltpu.roll(here, width - 1, 1))
    return lower, upper


def fill_slopes(t_ref, s_ref, also=None):
    depth, count, width = s_ref.shape[1:]

    @pl.loop(0, depth)
    def _(z):
        for j in range(count // ROWS):
            start = j * ROWS
            rows = pl.ds(start, ROWS)
            here = t_ref[z + 1, rows, :]
            y_low, y_high = beside_y(
                lambda at: t_ref[z + 1, pl.ds(at, 1), :], here, j == 0, start + ROWS == count, count, start
            )
            x_low, x_high = beside_x(here)
            s_ref[0, z, rows, :] = 0.5 * (t_ref[z + 2, rows, :] - t_ref[z, rows, :])
            s_ref[1, z, rows, :] = 0.5 * (y_high - y_low)
            s_ref[2, z, rows, :] = 0.5 * (x_high - x_low)
            if also is not None:
                also(z, rows)


def share_kernel(place, scale, t_hbm, parts_ref, out_ref, own_ref, sem):
    groups, count, width = parts_ref.shape
    copy = pltpu.make_async_copy(t_hbm.at[place[0]], own_ref, sem)
    copy.start()
    copy.wait()
    for j in range(count // ROWS):
        rows = pl.ds(j * ROWS, ROWS)
        value = parts_ref[0, rows, :]
        for g in range(1, groups):
            value = value + parts_ref[g, rows, :]
        if j * ROWS < own_ref.shape[0]:
            value = own_ref[rows, :] - scale * value
        for g in range(groups):
            out_ref[g, rows, :] = value


def finish_kernel(odd_ref, scale, all_ref, ti_hbm, to_hbm, out_ref, halo_ref, sem):
    depth, count, width = out_ref.shape
    pieces = depth // 2
    odd = odd_ref[0]
    copies = [
        pltpu.make_async_copy(far.at[far.shape[0] - 1], halo_ref.at[side], sem.at[side])
        for side, far in enumerate((ti_hbm, to_hbm))
    ]
    for copy in copies:
        copy.start()

    @pl.loop(0, depth)
    def _(z):
        out_ref[z] = all_ref[z, pl.ds(0, count), :]

    facing = jnp.where(odd == 1, 0, depth - 1)
    for side, z in enumerate((facing, depth - 1 - facing)):
        copies[side].wait()
        factor = jnp.where(z == 0, 0.5 * scale, -0.5 * scale)
        for q in range(pieces):
            rows = pl.ds(q * (count // pieces), count // pieces)
            speed = all_ref[jnp.where(z == 0, q, pieces + q), pl.ds(count, count // pieces), :]
            out_ref[z, rows, :] = out_ref[z, rows, :] + factor * halo_ref[side, rows, :] * speed


def move_kernel(
    odd_ref, cohort, gain, stiff, t_hbm, lab_hbm, im_hbm, v_hbm,
    sum_ref, inner_hbm, outer_hbm, out_hbm,
    t_ref, lab_ref, im_ref, v_ref, new_ref, s_ref, k_ref,
    t_sem, lab_sem, im_sem, v_sem, in_sem, far_sem, out_sem, face_sem,
):
    subjects, depth, count, width = im_ref.shape
    odd = odd_ref[0]
    template = [
        pltpu.make_async_copy(t_hbm, t_ref.at[pl.ds(1, depth)], t_sem),
        pltpu.make_async_copy(lab_hbm, lab_ref, lab_sem),
    ]
    facing = jnp.where(odd == 1, 0, depth - 1)
    half = depth // 2

    def arrivals(s):
        copies = [pltpu.make_async_copy(im_hbm.at[s], im_ref.at[s], im_sem.at[s])]
        for c in range(3):
            copies.append(
                pltpu.make_async_copy(v_hbm.at[s, c], v_ref.at[s, c, pl.ds(1, depth)], v_sem.at[s, c])
            )
        return copies

    def edges(s):
        return [
            pltpu.make_async_copy(v_ref.at[s, :, 1 + facing], inner_hbm.at[pl.ds(3 * s, 3)], in_sem.at[s]),
            pltpu.make_async_copy(v_ref.at[s, :, depth - facing], outer_hbm.at[pl.ds(3 * s, 3)], far_sem.at[s]),
        ]

    faces = [
        pltpu.make_async_copy(t_ref.at[1 + facing], inner_hbm.at[3 * subjects], face_sem.at[0]),
        pltpu.make_async_copy(t_ref.at[depth - facing], outer_hbm.at[3 * subjects], face_sem.at[1]),
    ]

    def departure(s, part):
        planes = pl.ds(part * half, half)
        return pltpu.make_async_copy(new_ref.at[s, :, planes], out_hbm.at[s, :, planes], out_sem.at[s, part])

    for copy in template:
        copy.start()
    ahead = min(AHEAD, subjects)
    for s in range(ahead):
        for copy in arrivals(s):
            copy.start()
    sum_ref[...] = jnp.zeros_like(sum_ref)
    outside = jnp.zeros((count, width), jnp.float32)
    t_ref[0] = outside
    t_ref[depth + 1] = outside

    @pl.loop(0, subjects)
    def _(s):
        for c in range(3):
            v_ref[s, c, 0] = outside
            v_ref[s, c, depth + 1] = outside

    for copy in template:
        copy.wait()
    for copy in faces:
        copy.start()

    def rate_of(z, rows):
        k_ref[z, rows, :] = rate_at(lab_ref[z, rows, :], stiff)

    fill_slopes(t_ref, s_ref, rate_of)

    @pl.loop(0, subjects)
    def _(s):
        for copy in arrivals(s):
            copy.wait()
        for copy in edges(s):
            copy.start()

        @pl.when(s + ahead < subjects)
        def _():
            for copy in arrivals(s + ahead):
                copy.start()

        level = gain[cohort[s]]

        def plane(z):
            force = jnp.where((z == 0) | (z == depth - 1), 0.0, velocity_step)
            for j in range(count // ROWS):
                start = j * ROWS
                rows = pl.ds(start, ROWS)
                field = [v_ref[s, c, z + 1, rows, :] for c in range(3)]
                slopes = [s_ref[c, z, rows, :] for c in range(3)]
                rate = k_ref[z, rows, :]
                value = t_ref[z + 1, rows, :] - level * im_ref[s, z, rows, :].astype(jnp.float32)
                for c in range(3):
                    value = value + slopes[c] * field[c]
                sum_ref[z, rows, :] = sum_ref[z, rows, :] + value
                value = force * value
                for c in range(3):
                    here = field[c]
                    y_low, y_high = beside_y(
                        lambda at: v_ref[s, c, z + 1, pl.ds(at, 1), :], here,
                        j == 0, start + ROWS == count, count, start,
                    )
                    x_low, x_high = beside_x(here)
                    around = (v_ref[s, c, z, rows, :] + v_ref[s, c, z + 2, rows, :]) + (y_low + y_high)
                    around = around + (x_low + x_high)
                    new_ref[s, c, z, rows, :] = here + rate * (around - 6.0 * here) - value * slopes[c]

        for part in range(2):
            pl.loop(part * half, (part + 1) * half)(plane)
            departure(s, part).start()

    piece = sum_ref.shape[1] - count
    for z, first in ((1, 0), (depth, depth // 2)):
        for q in range(depth // 2):
            rows = pl.ds(q * piece, piece)
            speed = v_ref[0, 0, z, rows, :]
            for s in range(1, subjects):
                speed = speed + v_ref[s, 0, z, rows, :]
            sum_ref[first + q, pl.ds(count, piece), :] = speed
    for copy in faces:
        copy.wait()

    @pl.loop(0, subjects)
    def _(s):
        for copy in edges(s):
            copy.wait()
        for part in range(2):
            departure(s, part).wait()


def rate_at(label, stiff):
    rate = jnp.full(label.shape, stiff[0], jnp.float32)
    for kind in range(1, stiff.shape[0]):
        rate = jnp.where(label == kind, stiff[kind], rate)
    return velocity_step * rate


def edge_kernel(
    odd_ref, cohort, gain, stiff, t_hbm, lab_hbm, im_hbm, own_in_hbm, own_far_hbm, vi_ref, vo_ref, old_hbm, out_hbm,
    t_ref, lab_ref, im_ref, own_ref, new_ref, s_ref, t_sem, lab_sem, im_sem, own_sem, get_sem, put_sem,
):
    subjects = im_ref.shape[1]
    depth, count, width = t_hbm.shape
    odd = odd_ref[0]
    facing = jnp.where(odd == 1, 0, depth - 1)
    sides = ((0, facing, vi_ref, own_in_hbm), (1, depth - 1 - facing, vo_ref, own_far_hbm))

    def early(side, z, own):
        beside = jnp.where(z == 0, 1, depth - 2)
        return [
            pltpu.make_async_copy(t_hbm.at[z], t_ref.at[side, 0], t_sem.at[side, 0]),
            pltpu.make_async_copy(t_hbm.at[beside], t_ref.at[side, 1], t_sem.at[side, 1]),
            pltpu.make_async_copy(lab_hbm.at[z], lab_ref.at[side], lab_sem.at[side]),
        ]

    def late(side, z, own, s):
        return [
            pltpu.make_async_copy(im_hbm.at[s, z], im_ref.at[side, s], im_sem.at[side, s]),
            pltpu.make_async_copy(own.at[pl.ds(3 * s, 3)], own_ref.at[side, s], own_sem.at[side, s]),
            pltpu.make_async_copy(old_hbm.at[s, :, z], new_ref.at[side, s], get_sem.at[side, s]),
        ]

    def store(side, z, s):
        return pltpu.make_async_copy(new_ref.at[side, s], out_hbm.at[s, :, z], put_sem.at[side, s])

    for side, z, _, own in sides:
        for copy in early(side, z, own):
            copy.start()
    for s in range(subjects):
        for side, z, _, own in sides:
            for copy in late(side, z, own, s):
                copy.start()
    for side, z, halo, own in sides:
        for copy in early(side, z, own):
            copy.wait()
        sign = jnp.where(z == 0, 0.5, -0.5)
        for j in range(count // ROWS):
            start = j * ROWS
            rows = pl.ds(start, ROWS)
            here = t_ref[side, 0, rows, :]
            y_low, y_high = beside_y(
                lambda at: t_ref[side, 0, pl.ds(at, 1), :], here, j == 0, start + ROWS == count, count, start
            )
            x_low, x_high = beside_x(here)
            s_ref[side, 0, rows, :] = sign * (t_ref[side, 1, rows, :] - halo[3 * subjects, rows, :])
            s_ref[side, 1, rows, :] = 0.5 * (y_high - y_low)
            s_ref[side, 2, rows, :] = 0.5 * (x_high - x_low)
            s_ref[side, 3, rows, :] = rate_at(lab_ref[side, rows, :], stiff)
    for s in range(subjects):
        level = gain[cohort[s]]
        for side, z, halo, own in sides:
            for copy in late(side, z, own, s):
                copy.wait()
            for j in range(count // ROWS):
                rows = pl.ds(j * ROWS, ROWS)
                value = t_ref[side, 0, rows, :] - level * im_ref[side, s, rows, :].astype(jnp.float32)
                for c in range(3):
                    value = value + s_ref[side, c, rows, :] * own_ref[side, s, c, rows, :]
                value = velocity_step * value
                rate = s_ref[side, 3, rows, :]
                for c in range(3):
                    new_ref[side, s, c, rows, :] = (
                        new_ref[side, s, c, rows, :]
                        + rate * halo[3 * s + c, rows, :]
                        - value * s_ref[side, c, rows, :]
                    )
            store(side, z, s).start()
    for s in range(subjects):
        for side, z, _, _ in sides:
            store(side, z, s).wait()


SMALL = pl.BlockSpec(memory_space=pltpu.SMEM)
FAR = pl.BlockSpec(memory_space=pltpu.HBM)
FREE = pl.BlockSpec(memory_space=pl.ANY)
NEAR = pl.BlockSpec(memory_space=pltpu.VMEM)
COPY = pltpu.SemaphoreType.DMA


def share_update(place, scale, template, parts):
    return pl.pallas_call(
        lambda *refs: share_kernel(refs[0], scale, *refs[1:]),
        out_shape=jax.ShapeDtypeStruct(parts.shape, jnp.float32),
        in_specs=[SMALL, FAR, NEAR],
        out_specs=NEAR,
        scratch_shapes=[pltpu.VMEM(template.shape[1:], jnp.float32), COPY(())],
        compiler_params=pltpu.CompilerParams(vmem_limit_bytes=8 * MIB),
        cost_estimate=pl.CostEstimate(flops=parts.size, bytes_accessed=2 * MIB, transcendentals=0),
        name="share_update",
    )(place, template, parts)


def moved(odd, cohort, gain, stiffness, template, labels, images, velocity, share_rows):
    subjects = images.shape[0]
    depth, count, width = template.shape
    edge = jax.ShapeDtypeStruct((3 * subjects + 1, count, width), jnp.float32)
    whole = jax.ShapeDtypeStruct(velocity.shape, jnp.float32)
    return pl.pallas_call(
        move_kernel,
        out_shape=[jax.ShapeDtypeStruct((depth, share_rows, width), jnp.float32), edge, edge, whole],
        in_specs=[SMALL] * 4 + [FAR] * 4,
        out_specs=[NEAR, FAR, FAR, FAR],
        scratch_shapes=[
            pltpu.VMEM((depth + 2, count, width), jnp.float32),
            pltpu.VMEM(labels.shape, labels.dtype),
            pltpu.VMEM(images.shape, images.dtype),
            pltpu.VMEM((subjects, 3, depth + 2, count, width), jnp.float32),
            pltpu.VMEM(velocity.shape, jnp.float32),
            pltpu.VMEM((3,) + template.shape, jnp.float32),
            pltpu.VMEM(template.shape, jnp.float32),
            COPY(()), COPY(()), COPY((subjects,)), COPY((subjects, 3)),
            COPY((subjects,)), COPY((subjects,)), COPY((subjects, 2)), COPY((2,)),
        ],
        compiler_params=pltpu.CompilerParams(vmem_limit_bytes=60 * MIB),
        cost_estimate=pl.CostEstimate(flops=8 * velocity.size, bytes_accessed=16 * MIB, transcendentals=0),
        name="moved",
    )(odd, cohort, gain, stiffness, template, labels, images, velocity)


def edges_added(odd, cohort, gain, stiffness, template, labels, images, inner, outer, v_inner, v_outer, velocity):
    subjects = images.shape[0]
    depth, count, width = template.shape
    return pl.pallas_call(
        edge_kernel,
        out_shape=jax.ShapeDtypeStruct(velocity.shape, jnp.float32),
        in_specs=[SMALL] * 4 + [FAR] * 5 + [NEAR, NEAR, FAR],
        out_specs=FAR,
        scratch_shapes=[
            pltpu.VMEM((2, 2, count, width), jnp.float32),
            pltpu.VMEM((2, count, width), labels.dtype),
            pltpu.VMEM((2, subjects, count, width), images.dtype),
            pltpu.VMEM((2, subjects, 3, count, width), jnp.float32),
            pltpu.VMEM((2, subjects, 3, count, width), jnp.float32),
            pltpu.VMEM((2, 4, count, width), jnp.float32),
            COPY((2, 2)), COPY((2,)), COPY((2, subjects)), COPY((2, subjects)), COPY((2, subjects)), COPY((2, subjects)),
        ],
        input_output_aliases={11: 0},
        compiler_params=pltpu.CompilerParams(vmem_limit_bytes=50 * MIB),
        cost_estimate=pl.CostEstimate(flops=velocity.size, bytes_accessed=8 * MIB, transcendentals=0),
        name="edges_added",
    )(odd, cohort, gain, stiffness, template, labels, images, inner, outer, v_inner, v_outer, velocity)


def finished(odd, scale, shares, t_inner, t_outer, shape):
    return pl.pallas_call(
        lambda *refs: finish_kernel(refs[0], scale, *refs[1:]),
        out_shape=jax.ShapeDtypeStruct(shape, jnp.float32),
        in_specs=[SMALL, NEAR, FREE, FREE],
        out_specs=NEAR,
        scratch_shapes=[pltpu.VMEM((2,) + shape[1:], jnp.float32), COPY((2,))],
        compiler_params=pltpu.CompilerParams(vmem_limit_bytes=8 * MIB),
        cost_estimate=pl.CostEstimate(flops=shares.size, bytes_accessed=2 * MIB, transcendentals=0),
        name="finished",
    )(odd, shares, t_inner, t_outer)


def local(template, images, velocity, labels, stiffness, cohort, site_gain):
    depth, count, _ = template.shape
    slabs = lax.axis_size("slab")
    groups = lax.axis_size("grp")
    assert depth == groups and slabs % 2 == 0 and 2 * count == ROWS * groups
    odd = (lax.axis_index("slab") % 2).reshape(1)
    place = lax.axis_index("grp").reshape(1)
    inside = [(i, i ^ 1) for i in range(slabs)]
    across = [(i, i + 1) for i in range(1, slabs - 1, 2)]
    across = across + [(target, source) for source, target in across]
    scale = template_step / (images.shape[0] * groups)
    part, inner, outer, new_velocity = moved(
        odd, cohort, site_gain, stiffness, template, labels, images, velocity, count + ROWS
    )
    v_inner = lax.ppermute(inner, "slab", inside)
    v_outer = lax.ppermute(outer, "slab", across)
    parts = lax.all_to_all(part, "grp", 0, 0, tiled=True)
    shares = share_update(place, scale, template, parts)
    shares = lax.all_to_all(shares, "grp", 0, 0, tiled=True)
    new_velocity = edges_added(
        odd, cohort, site_gain, stiffness, template, labels, images, inner, outer, v_inner, v_outer, new_velocity
    )
    new_template = finished(odd, scale, shares, v_inner, v_outer, template.shape)
    return (new_template, new_velocity)


def solution(mesh):
    placed = (
        P("slab", None, None),
        P("grp", "slab", None, None),
        P("grp", None, "slab", None, None),
        P("slab", None, None),
        P(),
        P("grp"),
        P(),
    )
    return jax.shard_map(
        local,
        mesh=mesh,
        in_specs=placed,
        out_specs=(P("slab", None, None), P("grp", None, "slab", None, None)),
        check_vma=False,
    )
```

```python
import jax
import jax.numpy as jnp
from jax import lax
from jax.experimental import pallas as pl
from jax.experimental.pallas import tpu as pltpu
from jax.sharding import PartitionSpec as P

velocity_step = 0.05
template_step = 0.5
ROWS = 16
AHEAD = 2
MIB = 1 << 20


def beside_y(get_row, here, first, last, count, start):
    rows, width = here.shape
    at = lax.broadcasted_iota(jnp.int32, (rows, width), 0)
    zero = jnp.zeros((rows, width), jnp.float32)
    before = zero if first else jnp.broadcast_to(get_row(start - 1), (rows, width))
    after = zero if last else jnp.broadcast_to(get_row(start + rows), (rows, width))
    lower = jnp.where(at == 0, before, pltpu.roll(here, 1, 0))
    upper = jnp.where(at == rows - 1, after, pltpu.roll(here, rows - 1, 0))
    return lower, upper


def beside_x(here):
    rows, width = here.shape
    at = lax.broadcasted_iota(jnp.int32, (rows, width), 1)
    zero = jnp.zeros((rows, width), jnp.float32)
    lower = jnp.where(at == 0, zero, pltpu.roll(here, 1, 1))
    upper = jnp.where(at == width - 1, zero, pltpu.roll(here, width - 1, 1))
    return lower, upper


def fill_slopes(t_ref, s_ref, also=None):
    depth, count, width = s_ref.shape[1:]

    @pl.loop(0, depth)
    def _(z):
        for j in range(count // ROWS):
            start = j * ROWS
            rows = pl.ds(start, ROWS)
            here = t_ref[z + 1, rows, :]
            y_low, y_high = beside_y(
                lambda at: t_ref[z + 1, pl.ds(at, 1), :], here, j == 0, start + ROWS == count, count, start
            )
            x_low, x_high = beside_x(here)
            s_ref[0, z, rows, :] = 0.5 * (t_ref[z + 2, rows, :] - t_ref[z, rows, :])
            s_ref[1, z, rows, :] = 0.5 * (y_high - y_low)
            s_ref[2, z, rows, :] = 0.5 * (x_high - x_low)
            if also is not None:
                also(z, rows)


def share_kernel(place, scale, t_hbm, parts_ref, out_ref, own_ref, sem):
    groups, count, width = parts_ref.shape
    copy = pltpu.make_async_copy(t_hbm.at[place[0]], own_ref, sem)
    copy.start()
    copy.wait()
    for j in range(count // ROWS):
        rows = pl.ds(j * ROWS, ROWS)
        value = parts_ref[0, rows, :]
        for g in range(1, groups):
            value = value + parts_ref[g, rows, :]
        if j * ROWS < own_ref.shape[0]:
            value = own_ref[rows, :] - scale * value
        for g in range(groups):
            out_ref[g, rows, :] = value


def finish_kernel(odd_ref, scale, all_ref, halo_ref, out_ref):
    depth, count, width = out_ref.shape
    pieces = depth // 2
    odd = odd_ref[0]

    @pl.loop(0, depth)
    def _(z):
        out_ref[z] = all_ref[z, pl.ds(0, count), :]

    facing = jnp.where(odd == 1, 0, depth - 1)
    for side, z in enumerate((facing, depth - 1 - facing)):
        factor = jnp.where(z == 0, 0.5 * scale, -0.5 * scale)
        for q in range(pieces):
            rows = pl.ds(q * (count // pieces), count // pieces)
            speed = all_ref[jnp.where(z == 0, q, pieces + q), pl.ds(count, count // pieces), :]
            out_ref[z, rows, :] = out_ref[z, rows, :] + factor * halo_ref[side, rows, :] * speed


def move_kernel(
    odd_ref, cohort, gain, stiff, t_hbm, lab_hbm, im_hbm, v_hbm,
    sum_ref, inner_hbm, outer_hbm, out_hbm,
    t_ref, lab_ref, im_ref, v_ref, new_ref, s_ref, k_ref,
    t_sem, lab_sem, im_sem, v_sem, in_sem, far_sem, out_sem, face_sem,
):
    subjects, depth, count, width = im_ref.shape
    odd = odd_ref[0]
    template = [
        pltpu.make_async_copy(t_hbm, t_ref.at[pl.ds(1, depth)], t_sem),
        pltpu.make_async_copy(lab_hbm, lab_ref, lab_sem),
    ]
    facing = jnp.where(odd == 1, 0, depth - 1)
    half = depth // 2

    def arrivals(s):
        copies = [pltpu.make_async_copy(im_hbm.at[s], im_ref.at[s], im_sem.at[s])]
        for c in range(3):
            copies.append(
                pltpu.make_async_copy(v_hbm.at[s, c], v_ref.at[s, c, pl.ds(1, depth)], v_sem.at[s, c])
            )
        return copies

    def edges(s):
        return [
            pltpu.make_async_copy(v_ref.at[s, :, 1 + facing], inner_hbm.at[pl.ds(3 * s, 3)], in_sem.at[s]),
            pltpu.make_async_copy(v_ref.at[s, :, depth - facing], outer_hbm.at[pl.ds(3 * s, 3)], far_sem.at[s]),
        ]

    faces = [
        pltpu.make_async_copy(t_ref.at[1 + facing], inner_hbm.at[3 * subjects], face_sem.at[0]),
        pltpu.make_async_copy(t_ref.at[depth - facing], outer_hbm.at[3 * subjects], face_sem.at[1]),
    ]

    def departure(s, part):
        planes = pl.ds(part * half, half)
        return pltpu.make_async_copy(new_ref.at[s, :, planes], out_hbm.at[s, :, planes], out_sem.at[s, part])

    for copy in template:
        copy.start()
    ahead = min(AHEAD, subjects)
    for s in range(ahead):
        for copy in arrivals(s):
            copy.start()
    sum_ref[...] = jnp.zeros_like(sum_ref)
    outside = jnp.zeros((count, width), jnp.float32)
    t_ref[0] = outside
    t_ref[depth + 1] = outside

    @pl.loop(0, subjects)
    def _(s):
        for c in range(3):
            v_ref[s, c, 0] = outside
            v_ref[s, c, depth + 1] = outside

    for copy in template:
        copy.wait()
    for copy in faces:
        copy.start()

    def rate_of(z, rows):
        k_ref[z, rows, :] = rate_at(lab_ref[z, rows, :], stiff)

    fill_slopes(t_ref, s_ref, rate_of)

    @pl.loop(0, subjects)
    def _(s):
        for copy in arrivals(s):
            copy.wait()
        for copy in edges(s):
            copy.start()

        @pl.when(s + ahead < subjects)
        def _():
            for copy in arrivals(s + ahead):
                copy.start()

        level = gain[cohort[s]]

        def plane(z):
            force = jnp.where((z == 0) | (z == depth - 1), 0.0, velocity_step)
            for j in range(count // ROWS):
                start = j * ROWS
                rows = pl.ds(start, ROWS)
                field = [v_ref[s, c, z + 1, rows, :] for c in range(3)]
                slopes = [s_ref[c, z, rows, :] for c in range(3)]
                rate = k_ref[z, rows, :]
                value = t_ref[z + 1, rows, :] - level * im_ref[s, z, rows, :].astype(jnp.float32)
                for c in range(3):
                    value = value + slopes[c] * field[c]
                sum_ref[z, rows, :] = sum_ref[z, rows, :] + value
                value = force * value
                for c in range(3):
                    here = field[c]
                    y_low, y_high = beside_y(
                        lambda at: v_ref[s, c, z + 1, pl.ds(at, 1), :], here,
                        j == 0, start + ROWS == count, count, start,
                    )
                    x_low, x_high = beside_x(here)
                    around = (v_ref[s, c, z, rows, :] + v_ref[s, c, z + 2, rows, :]) + (y_low + y_high)
                    around = around + (x_low + x_high)
                    new_ref[s, c, z, rows, :] = here + rate * (around - 6.0 * here) - value * slopes[c]

        for part in range(2):
            pl.loop(part * half, (part + 1) * half)(plane)
            departure(s, part).start()

    piece = sum_ref.shape[1] - count
    for z, first in ((1, 0), (depth, depth // 2)):
        for q in range(depth // 2):
            rows = pl.ds(q * piece, piece)
            speed = v_ref[0, 0, z, rows, :]
            for s in range(1, subjects):
                speed = speed + v_ref[s, 0, z, rows, :]
            sum_ref[first + q, pl.ds(count, piece), :] = speed
    for copy in faces:
        copy.wait()

    @pl.loop(0, subjects)
    def _(s):
        for copy in edges(s):
            copy.wait()
        for part in range(2):
            departure(s, part).wait()


def rate_at(label, stiff):
    rate = jnp.full(label.shape, stiff[0], jnp.float32)
    for kind in range(1, stiff.shape[0]):
        rate = jnp.where(label == kind, stiff[kind], rate)
    return velocity_step * rate


def edge_kernel(
    odd_ref, cohort, gain, stiff, t_hbm, lab_hbm, im_hbm, own_in_hbm, own_far_hbm, vi_hbm, vo_hbm, old_hbm, out_hbm, beyond_ref,
    t_ref, lab_ref, im_ref, own_ref, halo_ref, new_ref, s_ref,
    t_sem, lab_sem, im_sem, own_sem, halo_sem, get_sem, put_sem,
):
    subjects = im_ref.shape[1]
    depth, count, width = t_hbm.shape
    odd = odd_ref[0]
    facing = jnp.where(odd == 1, 0, depth - 1)
    sides = ((0, facing, vi_hbm, own_in_hbm), (1, depth - 1 - facing, vo_hbm, own_far_hbm))

    def early(side, z, halo):
        beside = jnp.where(z == 0, 1, depth - 2)
        return [
            pltpu.make_async_copy(t_hbm.at[z], t_ref.at[side, 0], t_sem.at[side, 0]),
            pltpu.make_async_copy(t_hbm.at[beside], t_ref.at[side, 1], t_sem.at[side, 1]),
            pltpu.make_async_copy(halo.at[3 * subjects], t_ref.at[side, 2], t_sem.at[side, 2]),
            pltpu.make_async_copy(lab_hbm.at[z], lab_ref.at[side], lab_sem.at[side]),
        ]

    def late(side, z, halo, own, s):
        return [
            pltpu.make_async_copy(im_hbm.at[s, z], im_ref.at[side, s], im_sem.at[side, s]),
            pltpu.make_async_copy(own.at[pl.ds(3 * s, 3)], own_ref.at[side, s], own_sem.at[side, s]),
            pltpu.make_async_copy(halo.at[pl.ds(3 * s, 3)], halo_ref.at[side, s], halo_sem.at[side, s]),
            pltpu.make_async_copy(old_hbm.at[s, :, z], new_ref.at[side, s], get_sem.at[side, s]),
        ]

    def store(side, z, s):
        return pltpu.make_async_copy(new_ref.at[side, s], out_hbm.at[s, :, z], put_sem.at[side, s])

    for side, z, halo, _ in sides:
        for copy in early(side, z, halo):
            copy.start()
    for s in range(subjects):
        for side, z, halo, own in sides:
            for copy in late(side, z, halo, own, s):
                copy.start()
    for side, z, halo, _ in sides:
        for copy in early(side, z, halo):
            copy.wait()
        sign = jnp.where(z == 0, 0.5, -0.5)
        beyond_ref[side] = t_ref[side, 2]
        for j in range(count // ROWS):
            start = j * ROWS
            rows = pl.ds(start, ROWS)
            here = t_ref[side, 0, rows, :]
            y_low, y_high = beside_y(
                lambda at: t_ref[side, 0, pl.ds(at, 1), :], here, j == 0, start + ROWS == count, count, start
            )
            x_low, x_high = beside_x(here)
            s_ref[side, 0, rows, :] = sign * (t_ref[side, 1, rows, :] - t_ref[side, 2, rows, :])
            s_ref[side, 1, rows, :] = 0.5 * (y_high - y_low)
            s_ref[side, 2, rows, :] = 0.5 * (x_high - x_low)
            s_ref[side, 3, rows, :] = rate_at(lab_ref[side, rows, :], stiff)
    for s in range(subjects):
        level = gain[cohort[s]]
        for side, z, halo, own in sides:
            for copy in late(side, z, halo, own, s):
                copy.wait()
            for j in range(count // ROWS):
                rows = pl.ds(j * ROWS, ROWS)
                value = t_ref[side, 0, rows, :] - level * im_ref[side, s, rows, :].astype(jnp.float32)
                for c in range(3):
                    value = value + s_ref[side, c, rows, :] * own_ref[side, s, c, rows, :]
                value = velocity_step * value
                rate = s_ref[side, 3, rows, :]
                for c in range(3):
                    new_ref[side, s, c, rows, :] = (
                        new_ref[side, s, c, rows, :]
                        + rate * halo_ref[side, s, c, rows, :]
                        - value * s_ref[side, c, rows, :]
                    )
            store(side, z, s).start()
    for s in range(subjects):
        for side, z, _, _ in sides:
            store(side, z, s).wait()


SMALL = pl.BlockSpec(memory_space=pltpu.SMEM)
FAR = pl.BlockSpec(memory_space=pltpu.HBM)
FREE = pl.BlockSpec(memory_space=pl.ANY)
NEAR = pl.BlockSpec(memory_space=pltpu.VMEM)
COPY = pltpu.SemaphoreType.DMA


def share_update(place, scale, template, parts):
    return pl.pallas_call(
        lambda *refs: share_kernel(refs[0], scale, *refs[1:]),
        out_shape=jax.ShapeDtypeStruct(parts.shape, jnp.float32),
        in_specs=[SMALL, FAR, NEAR],
        out_specs=NEAR,
        scratch_shapes=[pltpu.VMEM(template.shape[1:], jnp.float32), COPY(())],
        compiler_params=pltpu.CompilerParams(vmem_limit_bytes=8 * MIB),
        cost_estimate=pl.CostEstimate(flops=parts.size, bytes_accessed=2 * MIB, transcendentals=0),
        name="share_update",
    )(place, template, parts)


def moved(odd, cohort, gain, stiffness, template, labels, images, velocity, share_rows):
    subjects = images.shape[0]
    depth, count, width = template.shape
    edge = jax.ShapeDtypeStruct((3 * subjects + 1, count, width), jnp.float32)
    whole = jax.ShapeDtypeStruct(velocity.shape, jnp.float32)
    return pl.pallas_call(
        move_kernel,
        out_shape=[jax.ShapeDtypeStruct((depth, share_rows, width), jnp.float32), edge, edge, whole],
        in_specs=[SMALL] * 4 + [FAR] * 4,
        out_specs=[NEAR, FAR, FAR, FAR],
        scratch_shapes=[
            pltpu.VMEM((depth + 2, count, width), jnp.float32),
            pltpu.VMEM(labels.shape, labels.dtype),
            pltpu.VMEM(images.shape, images.dtype),
            pltpu.VMEM((subjects, 3, depth + 2, count, width), jnp.float32),
            pltpu.VMEM(velocity.shape, jnp.float32),
            pltpu.VMEM((3,) + template.shape, jnp.float32),
            pltpu.VMEM(template.shape, jnp.float32),
            COPY(()), COPY(()), COPY((subjects,)), COPY((subjects, 3)),
            COPY((subjects,)), COPY((subjects,)), COPY((subjects, 2)), COPY((2,)),
        ],
        compiler_params=pltpu.CompilerParams(vmem_limit_bytes=60 * MIB),
        cost_estimate=pl.CostEstimate(flops=8 * velocity.size, bytes_accessed=16 * MIB, transcendentals=0),
        name="moved",
    )(odd, cohort, gain, stiffness, template, labels, images, velocity)


def edges_added(odd, cohort, gain, stiffness, template, labels, images, inner, outer, v_inner, v_outer, velocity):
    subjects = images.shape[0]
    depth, count, width = template.shape
    return pl.pallas_call(
        edge_kernel,
        out_shape=[
            jax.ShapeDtypeStruct(velocity.shape, jnp.float32),
            jax.ShapeDtypeStruct((2, count, width), jnp.float32),
        ],
        in_specs=[SMALL] * 4 + [FAR] * 8,
        out_specs=[FAR, NEAR],
        scratch_shapes=[
            pltpu.VMEM((2, 3, count, width), jnp.float32),
            pltpu.VMEM((2, count, width), labels.dtype),
            pltpu.VMEM((2, subjects, count, width), images.dtype),
            pltpu.VMEM((2, subjects, 3, count, width), jnp.float32),
            pltpu.VMEM((2, subjects, 3, count, width), jnp.float32),
            pltpu.VMEM((2, subjects, 3, count, width), jnp.float32),
            pltpu.VMEM((2, 4, count, width), jnp.float32),
            COPY((2, 3)), COPY((2,)), COPY((2, subjects)), COPY((2, subjects)), COPY((2, subjects)), COPY((2, subjects)), COPY((2, subjects)),
        ],
        input_output_aliases={11: 0},
        compiler_params=pltpu.CompilerParams(vmem_limit_bytes=56 * MIB),
        cost_estimate=pl.CostEstimate(flops=velocity.size, bytes_accessed=8 * MIB, transcendentals=0),
        name="edges_added",
    )(odd, cohort, gain, stiffness, template, labels, images, inner, outer, v_inner, v_outer, velocity)


def finished(odd, scale, shares, halo, shape):
    return pl.pallas_call(
        lambda *refs: finish_kernel(refs[0], scale, *refs[1:]),
        out_shape=jax.ShapeDtypeStruct(shape, jnp.float32),
        in_specs=[SMALL, NEAR, NEAR],
        out_specs=NEAR,
        compiler_params=pltpu.CompilerParams(vmem_limit_bytes=8 * MIB),
        cost_estimate=pl.CostEstimate(flops=shares.size, bytes_accessed=2 * MIB, transcendentals=0),
        name="finished",
    )(odd, shares, halo)


def local(template, images, velocity, labels, stiffness, cohort, site_gain):
    depth, count, _ = template.shape
    slabs = lax.axis_size("slab")
    groups = lax.axis_size("grp")
    assert depth == groups and slabs % 2 == 0 and 2 * count == ROWS * groups
    odd = (lax.axis_index("slab") % 2).reshape(1)
    place = lax.axis_index("grp").reshape(1)
    inside = [(i, i ^ 1) for i in range(slabs)]
    across = [(i, i + 1) for i in range(1, slabs - 1, 2)]
    across = across + [(target, source) for source, target in across]
    scale = template_step / (images.shape[0] * groups)
    part, inner, outer, new_velocity = moved(
        odd, cohort, site_gain, stiffness, template, labels, images, velocity, count + ROWS
    )
    v_inner = lax.ppermute(inner, "slab", inside)
    v_outer = lax.ppermute(outer, "slab", across)
    parts = lax.all_to_all(part, "grp", 0, 0, tiled=True)
    shares = share_update(place, scale, template, parts)
    shares = lax.all_to_all(shares, "grp", 0, 0, tiled=True)
    new_velocity, halo = edges_added(
        odd, cohort, site_gain, stiffness, template, labels, images, inner, outer, v_inner, v_outer, new_velocity
    )
    new_template = finished(odd, scale, shares, halo, template.shape)
    return (new_template, new_velocity)


def solution(mesh):
    placed = (
        P("slab", None, None),
        P("grp", "slab", None, None),
        P("grp", None, "slab", None, None),
        P("slab", None, None),
        P(),
        P("grp"),
        P(),
    )
    return jax.shard_map(
        local,
        mesh=mesh,
        in_specs=placed,
        out_specs=(P("slab", None, None), P("grp", None, "slab", None, None)),
        check_vma=False,
    )
```

```python
import jax
import jax.numpy as jnp
from jax import lax
from jax.experimental import pallas as pl
from jax.experimental.pallas import tpu as pltpu
from jax.sharding import PartitionSpec as P

velocity_step = 0.05
template_step = 0.5
ROWS = 16
AHEAD = 2
MIB = 1 << 20


def beside_y(get_row, here, first, last, count, start):
    rows, width = here.shape
    at = lax.broadcasted_iota(jnp.int32, (rows, width), 0)
    zero = jnp.zeros((rows, width), jnp.float32)
    before = zero if first else jnp.broadcast_to(get_row(start - 1), (rows, width))
    after = zero if last else jnp.broadcast_to(get_row(start + rows), (rows, width))
    lower = jnp.where(at == 0, before, pltpu.roll(here, 1, 0))
    upper = jnp.where(at == rows - 1, after, pltpu.roll(here, rows - 1, 0))
    return lower, upper


def beside_x(here):
    rows, width = here.shape
    at = lax.broadcasted_iota(jnp.int32, (rows, width), 1)
    zero = jnp.zeros((rows, width), jnp.float32)
    lower = jnp.where(at == 0, zero, pltpu.roll(here, 1, 1))
    upper = jnp.where(at == width - 1, zero, pltpu.roll(here, width - 1, 1))
    return lower, upper


def fill_slopes(t_ref, s_ref, also=None):
    depth, count, width = s_ref.shape[1:]

    @pl.loop(0, depth)
    def _(z):
        for j in range(count // ROWS):
            start = j * ROWS
            rows = pl.ds(start, ROWS)
            here = t_ref[z + 1, rows, :]
            y_low, y_high = beside_y(
                lambda at: t_ref[z + 1, pl.ds(at, 1), :], here, j == 0, start + ROWS == count, count, start
            )
            x_low, x_high = beside_x(here)
            s_ref[0, z, rows, :] = 0.5 * (t_ref[z + 2, rows, :] - t_ref[z, rows, :])
            s_ref[1, z, rows, :] = 0.5 * (y_high - y_low)
            s_ref[2, z, rows, :] = 0.5 * (x_high - x_low)
            if also is not None:
                also(z, rows)


def share_kernel(place, scale, t_hbm, parts_ref, out_ref, own_ref, sem):
    groups, count, width = parts_ref.shape
    copy = pltpu.make_async_copy(t_hbm.at[place[0]], own_ref, sem)
    copy.start()
    copy.wait()
    for j in range(count // ROWS):
        rows = pl.ds(j * ROWS, ROWS)
        value = parts_ref[0, rows, :]
        for g in range(1, groups):
            value = value + parts_ref[g, rows, :]
        if j * ROWS < own_ref.shape[0]:
            value = own_ref[rows, :] - scale * value
        for g in range(groups):
            out_ref[g, rows, :] = value


def finish_kernel(odd_ref, scale, all_ref, halo_ref, out_ref):
    depth, count, width = out_ref.shape
    pieces = depth // 2
    odd = odd_ref[0]

    @pl.loop(0, depth)
    def _(z):
        out_ref[z] = all_ref[z, pl.ds(0, count), :]

    facing = jnp.where(odd == 1, 0, depth - 1)
    for side, z in enumerate((facing, depth - 1 - facing)):
        factor = jnp.where(z == 0, 0.5 * scale, -0.5 * scale)
        for q in range(pieces):
            rows = pl.ds(q * (count // pieces), count // pieces)
            speed = all_ref[jnp.where(z == 0, q, pieces + q), pl.ds(count, count // pieces), :]
            out_ref[z, rows, :] = out_ref[z, rows, :] + factor * halo_ref[side, rows, :] * speed


def move_kernel(
    odd_ref, cohort, gain, stiff, t_hbm, lab_hbm, im_hbm, v_hbm,
    sum_ref, inner_hbm, outer_hbm, out_hbm,
    t_ref, lab_ref, im_ref, v_ref, new_ref, s_ref, k_ref,
    t_sem, lab_sem, im_sem, v_sem, in_sem, far_sem, out_sem, face_sem,
):
    subjects, depth, count, width = im_ref.shape
    odd = odd_ref[0]
    template = [
        pltpu.make_async_copy(t_hbm, t_ref.at[pl.ds(1, depth)], t_sem),
        pltpu.make_async_copy(lab_hbm, lab_ref, lab_sem),
    ]
    facing = jnp.where(odd == 1, 0, depth - 1)
    half = depth // 2

    def arrivals(s):
        copies = [pltpu.make_async_copy(im_hbm.at[s], im_ref.at[s], im_sem.at[s])]
        for c in range(3):
            copies.append(
                pltpu.make_async_copy(v_hbm.at[s, c], v_ref.at[s, c, pl.ds(1, depth)], v_sem.at[s, c])
            )
        return copies

    def edges(s):
        return [
            pltpu.make_async_copy(v_ref.at[s, :, 1 + facing], inner_hbm.at[pl.ds(3 * s, 3)], in_sem.at[s]),
            pltpu.make_async_copy(v_ref.at[s, :, depth - facing], outer_hbm.at[pl.ds(3 * s, 3)], far_sem.at[s]),
        ]

    faces = [
        pltpu.make_async_copy(t_ref.at[1 + facing], inner_hbm.at[3 * subjects], face_sem.at[0]),
        pltpu.make_async_copy(t_ref.at[depth - facing], outer_hbm.at[3 * subjects], face_sem.at[1]),
    ]

    def departure(s, part):
        planes = pl.ds(part * half, half)
        return pltpu.make_async_copy(new_ref.at[s, :, planes], out_hbm.at[s, :, planes], out_sem.at[s, part])

    for copy in template:
        copy.start()
    ahead = min(AHEAD, subjects)
    for s in range(ahead):
        for copy in arrivals(s):
            copy.start()
    sum_ref[...] = jnp.zeros_like(sum_ref)
    outside = jnp.zeros((count, width), jnp.float32)
    t_ref[0] = outside
    t_ref[depth + 1] = outside

    @pl.loop(0, subjects)
    def _(s):
        for c in range(3):
            v_ref[s, c, 0] = outside
            v_ref[s, c, depth + 1] = outside

    for copy in template:
        copy.wait()
    for copy in faces:
        copy.start()

    def rate_of(z, rows):
        k_ref[z, rows, :] = rate_at(lab_ref[z, rows, :], stiff)

    fill_slopes(t_ref, s_ref, rate_of)

    @pl.loop(0, subjects)
    def _(s):
        for copy in arrivals(s):
            copy.wait()
        for copy in edges(s):
            copy.start()

        @pl.when(s + ahead < subjects)
        def _():
            for copy in arrivals(s + ahead):
                copy.start()

        level = gain[cohort[s]]

        def plane(z):
            force = jnp.where((z == 0) | (z == depth - 1), 0.0, velocity_step)
            for j in range(count // ROWS):
                start = j * ROWS
                rows = pl.ds(start, ROWS)
                field = [v_ref[s, c, z + 1, rows, :] for c in range(3)]
                slopes = [s_ref[c, z, rows, :] for c in range(3)]
                rate = k_ref[z, rows, :]
                value = t_ref[z + 1, rows, :] - level * im_ref[s, z, rows, :].astype(jnp.float32)
                for c in range(3):
                    value = value + slopes[c] * field[c]
                sum_ref[z, rows, :] = sum_ref[z, rows, :] + value
                value = force * value
                for c in range(3):
                    here = field[c]
                    y_low, y_high = beside_y(
                        lambda at: v_ref[s, c, z + 1, pl.ds(at, 1), :], here,
                        j == 0, start + ROWS == count, count, start,
                    )
                    x_low, x_high = beside_x(here)
                    around = (v_ref[s, c, z, rows, :] + v_ref[s, c, z + 2, rows, :]) + (y_low + y_high)
                    around = around + (x_low + x_high)
                    new_ref[s, c, z, rows, :] = here + rate * (around - 6.0 * here) - value * slopes[c]

        for part in range(2):
            pl.loop(part * half, (part + 1) * half)(plane)
            departure(s, part).start()

    piece = sum_ref.shape[1] - count
    for z, first in ((1, 0), (depth, depth // 2)):
        for q in range(depth // 2):
            rows = pl.ds(q * piece, piece)
            speed = v_ref[0, 0, z, rows, :]
            for s in range(1, subjects):
                speed = speed + v_ref[s, 0, z, rows, :]
            sum_ref[first + q, pl.ds(count, piece), :] = speed
    for copy in faces:
        copy.wait()

    @pl.loop(0, subjects)
    def _(s):
        for copy in edges(s):
            copy.wait()
        for part in range(2):
            departure(s, part).wait()


def rate_at(label, stiff):
    rate = jnp.full(label.shape, stiff[0], jnp.float32)
    for kind in range(1, stiff.shape[0]):
        rate = jnp.where(label == kind, stiff[kind], rate)
    return velocity_step * rate


def edge_kernel(
    odd_ref, cohort, gain, stiff, t_hbm, lab_hbm, im_hbm, own_in_hbm, own_far_hbm, vi_hbm, vo_hbm, old_hbm, out_hbm,
    t_ref, lab_ref, im_ref, own_ref, halo_ref, new_ref, s_ref,
    t_sem, lab_sem, im_sem, own_sem, halo_sem, get_sem, put_sem,
):
    subjects = im_ref.shape[1]
    depth, count, width = t_hbm.shape
    odd = odd_ref[0]
    facing = jnp.where(odd == 1, 0, depth - 1)
    sides = ((0, facing, vi_hbm, own_in_hbm), (1, depth - 1 - facing, vo_hbm, own_far_hbm))

    def early(side, z, halo):
        beside = jnp.where(z == 0, 1, depth - 2)
        return [
            pltpu.make_async_copy(t_hbm.at[z], t_ref.at[side, 0], t_sem.at[side, 0]),
            pltpu.make_async_copy(t_hbm.at[beside], t_ref.at[side, 1], t_sem.at[side, 1]),
            pltpu.make_async_copy(halo.at[3 * subjects], t_ref.at[side, 2], t_sem.at[side, 2]),
            pltpu.make_async_copy(lab_hbm.at[z], lab_ref.at[side], lab_sem.at[side]),
        ]

    def late(side, z, halo, own, s):
        return [
            pltpu.make_async_copy(im_hbm.at[s, z], im_ref.at[side, s], im_sem.at[side, s]),
            pltpu.make_async_copy(own.at[pl.ds(3 * s, 3)], own_ref.at[side, s], own_sem.at[side, s]),
            pltpu.make_async_copy(halo.at[pl.ds(3 * s, 3)], halo_ref.at[side, s], halo_sem.at[side, s]),
            pltpu.make_async_copy(old_hbm.at[s, :, z], new_ref.at[side, s], get_sem.at[side, s]),
        ]

    def store(side, z, s):
        return pltpu.make_async_copy(new_ref.at[side, s], out_hbm.at[s, :, z], put_sem.at[side, s])

    for side, z, halo, _ in sides:
        for copy in early(side, z, halo):
            copy.start()
    for s in range(subjects):
        for side, z, halo, own in sides:
            for copy in late(side, z, halo, own, s):
                copy.start()
    for side, z, halo, _ in sides:
        for copy in early(side, z, halo):
            copy.wait()
        sign = jnp.where(z == 0, 0.5, -0.5)
        for j in range(count // ROWS):
            start = j * ROWS
            rows = pl.ds(start, ROWS)
            here = t_ref[side, 0, rows, :]
            y_low, y_high = beside_y(
                lambda at: t_ref[side, 0, pl.ds(at, 1), :], here, j == 0, start + ROWS == count, count, start
            )
            x_low, x_high = beside_x(here)
            s_ref[side, 0, rows, :] = sign * (t_ref[side, 1, rows, :] - t_ref[side, 2, rows, :])
            s_ref[side, 1, rows, :] = 0.5 * (y_high - y_low)
            s_ref[side, 2, rows, :] = 0.5 * (x_high - x_low)
            s_ref[side, 3, rows, :] = rate_at(lab_ref[side, rows, :], stiff)
    for s in range(subjects):
        level = gain[cohort[s]]
        for side, z, halo, own in sides:
            for copy in late(side, z, halo, own, s):
                copy.wait()
            for j in range(count // ROWS):
                rows = pl.ds(j * ROWS, ROWS)
                value = t_ref[side, 0, rows, :] - level * im_ref[side, s, rows, :].astype(jnp.float32)
                for c in range(3):
                    value = value + s_ref[side, c, rows, :] * own_ref[side, s, c, rows, :]
                value = velocity_step * value
                rate = s_ref[side, 3, rows, :]
                for c in range(3):
                    new_ref[side, s, c, rows, :] = (
                        new_ref[side, s, c, rows, :]
                        + rate * halo_ref[side, s, c, rows, :]
                        - value * s_ref[side, c, rows, :]
                    )
            store(side, z, s).start()
    for s in range(subjects):
        for side, z, _, _ in sides:
            store(side, z, s).wait()


SMALL = pl.BlockSpec(memory_space=pltpu.SMEM)
FAR = pl.BlockSpec(memory_space=pltpu.HBM)
FREE = pl.BlockSpec(memory_space=pl.ANY)
NEAR = pl.BlockSpec(memory_space=pltpu.VMEM)
COPY = pltpu.SemaphoreType.DMA


def share_update(place, scale, template, parts):
    return pl.pallas_call(
        lambda *refs: share_kernel(refs[0], scale, *refs[1:]),
        out_shape=jax.ShapeDtypeStruct(parts.shape, jnp.float32),
        in_specs=[SMALL, FAR, NEAR],
        out_specs=NEAR,
        scratch_shapes=[pltpu.VMEM(template.shape[1:], jnp.float32), COPY(())],
        compiler_params=pltpu.CompilerParams(vmem_limit_bytes=8 * MIB),
        cost_estimate=pl.CostEstimate(flops=parts.size, bytes_accessed=2 * MIB, transcendentals=0),
        name="share_update",
    )(place, template, parts)


def moved(odd, cohort, gain, stiffness, template, labels, images, velocity, share_rows):
    subjects = images.shape[0]
    depth, count, width = template.shape
    edge = jax.ShapeDtypeStruct((3 * subjects + 1, count, width), jnp.float32)
    whole = jax.ShapeDtypeStruct(velocity.shape, jnp.float32)
    return pl.pallas_call(
        move_kernel,
        out_shape=[jax.ShapeDtypeStruct((depth, share_rows, width), jnp.float32), edge, edge, whole],
        in_specs=[SMALL] * 4 + [FAR] * 4,
        out_specs=[NEAR, FAR, FAR, FAR],
        scratch_shapes=[
            pltpu.VMEM((depth + 2, count, width), jnp.float32),
            pltpu.VMEM(labels.shape, labels.dtype),
            pltpu.VMEM(images.shape, images.dtype),
            pltpu.VMEM((subjects, 3, depth + 2, count, width), jnp.float32),
            pltpu.VMEM(velocity.shape, jnp.float32),
            pltpu.VMEM((3,) + template.shape, jnp.float32),
            pltpu.VMEM(template.shape, jnp.float32),
            COPY(()), COPY(()), COPY((subjects,)), COPY((subjects, 3)),
            COPY((subjects,)), COPY((subjects,)), COPY((subjects, 2)), COPY((2,)),
        ],
        compiler_params=pltpu.CompilerParams(vmem_limit_bytes=60 * MIB),
        cost_estimate=pl.CostEstimate(flops=8 * velocity.size, bytes_accessed=16 * MIB, transcendentals=0),
        name="moved",
    )(odd, cohort, gain, stiffness, template, labels, images, velocity)


def edges_added(odd, cohort, gain, stiffness, template, labels, images, inner, outer, v_inner, v_outer, velocity):
    subjects = images.shape[0]
    depth, count, width = template.shape
    return pl.pallas_call(
        edge_kernel,
        out_shape=jax.ShapeDtypeStruct(velocity.shape, jnp.float32),
        in_specs=[SMALL] * 4 + [FAR] * 8,
        out_specs=FAR,
        scratch_shapes=[
            pltpu.VMEM((2, 3, count, width), jnp.float32),
            pltpu.VMEM((2, count, width), labels.dtype),
            pltpu.VMEM((2, subjects, count, width), images.dtype),
            pltpu.VMEM((2, subjects, 3, count, width), jnp.float32),
            pltpu.VMEM((2, subjects, 3, count, width), jnp.float32),
            pltpu.VMEM((2, subjects, 3, count, width), jnp.float32),
            pltpu.VMEM((2, 4, count, width), jnp.float32),
            COPY((2, 3)), COPY((2,)), COPY((2, subjects)), COPY((2, subjects)), COPY((2, subjects)), COPY((2, subjects)), COPY((2, subjects)),
        ],
        input_output_aliases={11: 0},
        compiler_params=pltpu.CompilerParams(vmem_limit_bytes=56 * MIB),
        cost_estimate=pl.CostEstimate(flops=velocity.size, bytes_accessed=8 * MIB, transcendentals=0),
        name="edges_added",
    )(odd, cohort, gain, stiffness, template, labels, images, inner, outer, v_inner, v_outer, velocity)


def finished(odd, scale, shares, halo, shape):
    return pl.pallas_call(
        lambda *refs: finish_kernel(refs[0], scale, *refs[1:]),
        out_shape=jax.ShapeDtypeStruct(shape, jnp.float32),
        in_specs=[SMALL, NEAR, NEAR],
        out_specs=NEAR,
        compiler_params=pltpu.CompilerParams(vmem_limit_bytes=8 * MIB),
        cost_estimate=pl.CostEstimate(flops=shares.size, bytes_accessed=2 * MIB, transcendentals=0),
        name="finished",
    )(odd, shares, halo)


def local(template, images, velocity, labels, stiffness, cohort, site_gain):
    depth, count, _ = template.shape
    slabs = lax.axis_size("slab")
    groups = lax.axis_size("grp")
    assert depth == groups and slabs % 2 == 0 and 2 * count == ROWS * groups
    odd = (lax.axis_index("slab") % 2).reshape(1)
    place = lax.axis_index("grp").reshape(1)
    inside = [(i, i ^ 1) for i in range(slabs)]
    across = [(i, i + 1) for i in range(1, slabs - 1, 2)]
    across = across + [(target, source) for source, target in across]
    scale = template_step / (images.shape[0] * groups)
    part, inner, outer, new_velocity = moved(
        odd, cohort, site_gain, stiffness, template, labels, images, velocity, count + ROWS
    )
    v_inner = lax.ppermute(inner, "slab", inside)
    v_outer = lax.ppermute(outer, "slab", across)
    parts = lax.all_to_all(part, "grp", 0, 0, tiled=True)
    shares = share_update(place, scale, template, parts)
    shares = lax.all_to_all(shares, "grp", 0, 0, tiled=True)
    new_velocity = edges_added(
        odd, cohort, site_gain, stiffness, template, labels, images, inner, outer, v_inner, v_outer, new_velocity
    )
    new_template = finished(odd, scale, shares, jnp.stack([v_inner[-1], v_outer[-1]]), template.shape)
    return (new_template, new_velocity)


def solution(mesh):
    placed = (
        P("slab", None, None),
        P("grp", "slab", None, None),
        P("grp", None, "slab", None, None),
        P("slab", None, None),
        P(),
        P("grp"),
        P(),
    )
    return jax.shard_map(
        local,
        mesh=mesh,
        in_specs=placed,
        out_specs=(P("slab", None, None), P("grp", None, "slab", None, None)),
        check_vma=False,
    )
```
